32 devices in a mesh: bins: 2 (over x), fsdp: 16 (over z, y, core).
Axes of the slice: x: 2, y: 2, z: 4, core: 2. Of those that a mesh axis runs over, the one named last changes fastest.
Arguments:
- tokens: bfloat16 [16384, 1152], P(('bins', 'fsdp')), may hold values from -6 to 6
- condition: float32 [2, 1152], P('bins'), may hold values from -6 to 6
- segments: int32 [16384], P('bins'), may hold values from 0 to 63, as said below
- cotangent: bfloat16 [16384, 1152], P(('bins', 'fsdp')), may hold values from -6 to 6
- target: bfloat16 [16384, 768], P(('bins', 'fsdp')), may hold values from -6 to 6
- w_ada: bfloat16 [1152, 6912], P(None, 'fsdp'), may hold values from -0.1875 to 0.1875
- w_qkv: bfloat16 [1152, 3456], P('fsdp'), may hold values from -0.1875 to 0.1875
- w_out: bfloat16 [1152, 1152], P('fsdp'), may hold values from -0.75 to 0.75
- w_fc1: bfloat16 [1152, 4608], P('fsdp'), may hold values from -0.1875 to 0.1875
- w_fc2: bfloat16 [4608, 1152], P('fsdp'), may hold values from -0.09375 to 0.09375
- w_proj1: bfloat16 [1152, 2048], P('fsdp'), may hold values from -0.1875 to 0.1875
- w_proj2: bfloat16 [2048, 2048], P('fsdp'), may hold values from -0.125 to 0.125
- w_proj3: bfloat16 [2048, 768], P('fsdp'), may hold values from -0.125 to 0.125
Outputs:
- output: bfloat16 [16384, 1152], P(('bins', 'fsdp'))
- grad_tokens: float32 [16384, 1152], P(('bins', 'fsdp'))
- grad_condition: float32 [2, 1152], P('bins')
- grad_ada: float32 [1152, 6912], P(None, 'fsdp')
- grad_qkv: float32 [1152, 3456], P('fsdp')
- grad_out: float32 [1152, 1152], P('fsdp')
- grad_fc1: float32 [1152, 4608], P('fsdp')
- grad_fc2: float32 [4608, 1152], P('fsdp')
- grad_proj1: float32 [1152, 2048], P('fsdp')
- grad_proj2: float32 [2048, 2048], P('fsdp')
- grad_proj3: float32 [2048, 768], P('fsdp')
The draws below stay inside these ranges and needn't reach their ends.
Inputs may be any that keep to these rules, and one draw needn't show every extreme that they name: segments never fall; each aligned block of 1024 tokens holds either one image of 1024 tokens or four images of 256 tokens; images of different blocks have different ids; the first block holds one image and the last block four.
All inputs are finite; a program needn't handle non-finite values.
Results may differ from the reference program's by a relative error of at most 0.015.
Values may be sent and summed in bfloat16 or wider, within the bound.
No kernel may reach another device: no remote copies, remote signals or barrier semaphores. Data moves between devices by JAX's collectives and lax.ppermute only.
A program may use at most 320 MiB of HBM per device.

```python
import jax
import jax.numpy as jnp
from jax import lax

D = 1152
HEADS = 16
FF = 4608
MOD = 6912
PROJ = 2048
TARGET = 768
TOK_DEV = 512
SHORT = 256
TOKENS = 16384
N_BINS = 2


def draw_segments(key, part):
    pairs = TOKENS // (2 * TOK_DEV)
    longbits = jax.random.randint(key, (pairs,), 0, 2)
    longbits = longbits.at[0].set(1).at[pairs - 1].set(0)
    position = jnp.arange(TOKENS, dtype=jnp.int32)
    which = position // (2 * TOK_DEV)
    inside = position % (2 * TOK_DEV)
    picked = jnp.take(longbits, which)
    return (4 * which + jnp.where(picked == 1, 0, inside // SHORT)).astype(jnp.int32)


def block_levels(own_key, dims, pieces, least, top_value):
    def one(dim, shards_of):
        draws = jax.random.uniform(jax.random.fold_in(jax.random.fold_in(own_key, 6), dim), (shards_of,), jnp.float32, least / len(pieces), top_value / len(pieces))
        return jnp.repeat(jnp.exp(draws), dims[dim] // shards_of).reshape((-1,) + (1,) * (len(dims) - dim - 1))

    level = one(*pieces[0])
    for cut in pieces[1:]:
        level = level * one(*cut)
    return level


def bell_draw(rng, dims, deviation, bound, split=(), kind=jnp.bfloat16):
    loudness = block_levels(rng, dims, split, -0.22, 0.18) if split else 1.0
    entries = jax.random.normal(rng, dims, jnp.float32) * deviation * loudness
    return jnp.minimum(jnp.maximum(entries, -bound), bound).astype(kind)


def setup_inputs(seed: int = 0) -> dict:
    splits = jax.random.split(jax.random.key(seed), 14)
    return {
        "tokens": bell_draw(splits[0], (TOKENS, D), 1.0, 6.0, ((0, 32),)),
        "condition": bell_draw(splits[1], (N_BINS, D), 1.0, 6.0, ((0, 2),), jnp.float32),
        "segments": draw_segments(jax.random.fold_in(splits[13], 71), 0),
        "cotangent": bell_draw(splits[3], (TOKENS, D), 1.0, 6.0, ((0, 32),)),
        "target": bell_draw(splits[4], (TOKENS, TARGET), 1.0, 6.0, ((0, 32),)),
        "w_ada": bell_draw(splits[5], (D, MOD), D ** -0.5, 0.1875, ((1, 16),)),
        "w_qkv": bell_draw(splits[6], (D, 3 * D), D ** -0.5, 0.1875, ((0, 16),)),
        "w_out": bell_draw(splits[7], (D, D), (D // 16) ** -0.5, 0.75, ((0, 16),)),
        "w_fc1": bell_draw(splits[8], (D, FF), D ** -0.5, 0.1875, ((0, 16),)),
        "w_fc2": bell_draw(splits[9], (FF, D), FF ** -0.5, 0.09375, ((0, 16),)),
        "w_proj1": bell_draw(splits[10], (D, PROJ), D ** -0.5, 0.1875, ((0, 16),)),
        "w_proj2": bell_draw(splits[11], (PROJ, PROJ), PROJ ** -0.5, 0.125, ((0, 16),)),
        "w_proj3": bell_draw(splits[12], (PROJ, TARGET), PROJ ** -0.5, 0.125, ((0, 16),)),
    }


HIGH = lax.Precision.HIGHEST

@jax.custom_vjp
def low(v):
    return lax.optimization_barrier(v.astype(jnp.bfloat16)).astype(jnp.float32)

@jax.custom_vjp
def low_back(v):
    return v

def low_keep(v):
    return (low(v), None)

def low_pass(kept, grad):
    return (grad,)

def back_keep(v):
    return (v, None)

def back_low(kept, grad):
    return (low(grad),)
low.defvjp(low_keep, low_pass)
low_back.defvjp(back_keep, back_low)

def modulate(values, shift, scale):
    center = values - lax.optimization_barrier(jnp.mean(values, axis=-1, keepdims=True))
    spread = lax.optimization_barrier(jnp.mean(center * center, axis=-1, keepdims=True))
    return center * lax.rsqrt(spread + 1e-06) * (1.0 + scale) + shift

def cosine_sum(target_f, predicted):
    dots = lax.optimization_barrier(jnp.sum(predicted * target_f, axis=-1))
    first = lax.rsqrt(lax.optimization_barrier(jnp.sum(predicted * predicted, axis=-1)) + 1e-06)
    second = lax.rsqrt(lax.optimization_barrier(jnp.sum(target_f * target_f, axis=-1)) + 1e-06)
    return jnp.sum(dots * first * second)

def matmul(left, right):
    return jnp.dot(left, right, precision=HIGH)

def attend_block(operands):
    queries, keys, values, labels = operands
    head_size = queries.shape[-1]
    raw = jnp.einsum('qhd,khd->hqk', queries, keys, precision=HIGH) * head_size ** (-0.5)
    raw = low_back(raw)
    same = labels[:, None] == labels[None, :]
    masked = jnp.where(same[None], raw, -1e+30)
    probs = jax.nn.softmax(masked, axis=-1)
    return jnp.einsum('hqk,khd->qhd', low(probs), values, precision=HIGH)

def forward(tokens_f, cond_f, w_ada, w_qkv, w_out, w_fc1, w_fc2, w_proj1, w_proj2, w_proj3, segments, target_f):
    groups = N_BINS
    group_rows = TOKENS // groups
    blocks = TOKENS // (2 * TOK_DEV)
    width = D
    head_size = D // HEADS
    modulation = matmul(low(jax.nn.silu(cond_f)), w_ada).reshape(groups, 6, 1, width)
    grouped = tokens_f.reshape(groups, group_rows, width)
    h_one = low(modulate(grouped, modulation[:, 0], modulation[:, 1]))
    qkv = low(low_back(matmul(h_one.reshape(TOKENS, width), w_qkv)))
    qkv = qkv.reshape(blocks, 2 * TOK_DEV, 3, HEADS, head_size)
    attended = lax.map(jax.checkpoint(attend_block), (qkv[:, :, 0], qkv[:, :, 1], qkv[:, :, 2], segments.reshape(blocks, 2 * TOK_DEV)))
    attended = low(low_back(attended)).reshape(TOKENS, width)
    branch_one = low_back(matmul(attended, w_out)).reshape(groups, group_rows, width)
    resid_one = grouped + modulation[:, 2] * branch_one
    h_two = low(modulate(resid_one, modulation[:, 3], modulation[:, 4])).reshape(TOKENS, width)
    hidden_pre = low_back(matmul(h_two, w_fc1))
    hidden = low(jax.nn.gelu(hidden_pre, approximate=True))
    branch_two = low_back(matmul(hidden, w_fc2)).reshape(groups, group_rows, width)
    result = resid_one + modulation[:, 5] * branch_two
    result_low = low(result).reshape(TOKENS, width)
    first = low(jax.nn.silu(low_back(matmul(result_low, w_proj1))))
    second = low(jax.nn.silu(low_back(matmul(first, w_proj2))))
    predicted = low_back(matmul(second, w_proj3))
    return (result_low, cosine_sum(target_f, predicted))

def reference(tokens, condition, segments, cotangent, target, w_ada, w_qkv, w_out, w_fc1, w_fc2, w_proj1, w_proj2, w_proj3):
    target_f = target.astype(jnp.float32)
    inputs = (tokens.astype(jnp.float32), condition.astype(jnp.float32), w_ada.astype(jnp.float32), w_qkv.astype(jnp.float32), w_out.astype(jnp.float32), w_fc1.astype(jnp.float32), w_fc2.astype(jnp.float32), w_proj1.astype(jnp.float32), w_proj2.astype(jnp.float32), w_proj3.astype(jnp.float32))

    def wrapped(*values):
        return forward(*values, segments, target_f)
    outputs, pullback = jax.vjp(wrapped, *inputs)
    grads = pullback((cotangent.astype(jnp.float32), jnp.float32(-1.0)))
    return (outputs[0].astype(jnp.bfloat16), grads[0], grads[1], grads[2], grads[3], grads[4], grads[5], grads[6], grads[7], grads[8], grads[9])
```

```python
from functools import partial

import jax
import jax.numpy as jnp
from jax import lax
from jax.sharding import PartitionSpec as P

HEADS = 16


HIGH = lax.Precision.HIGHEST


def swapped(block, axis, apart):
    count = lax.axis_size(axis)
    route = []
    for low in range(count):
        high = low | 1 << apart
        if high != low and high < count:
            route += [(low, high), (high, low)]
    return lax.ppermute(block, axis, route)


def bins_peer(block):
    return lax.ppermute(block, "bins", [(0, 1), (1, 0)])


def hop(block, apart):
    chips = lax.axis_size("fsdp") // 2
    route = [2 * chip for chip in range(chips // 2)]
    route = route + [chip + 1 for chip in reversed(route)]
    pairs = []
    for spot, chip in enumerate(route):
        onward = route[(spot + apart) % chips]
        pairs += [(2 * chip, 2 * onward), (2 * chip + 1, 2 * onward + 1)]
    return lax.ppermute(block, "fsdp", pairs)


def chip_at(apart):
    chips = lax.axis_size("fsdp") // 2
    chip = lax.axis_index("fsdp") // 2
    spot = jnp.where(chip % 2 == 0, chip // 2, chips - 1 - chip // 2)
    spot = (spot + apart) % chips
    return jnp.where(spot < chips // 2, 2 * spot, 2 * (chips - 1 - spot) + 1)


def doubled(block):
    count, place = lax.axis_size("fsdp"), lax.axis_index("fsdp")
    step = 0
    while 1 << step < count:
        other = swapped(block, "fsdp", step)
        upper = (place >> step) % 2 == 1
        block = jnp.where(
            upper, jnp.concatenate([other, block]), jnp.concatenate([block, other])
        )
        step += 1
    return block


def halved(block):
    count, place = lax.axis_size("fsdp"), lax.axis_index("fsdp")
    step = count.bit_length() - 1
    while step:
        step -= 1
        upper = (place >> step) % 2
        length = block.shape[0] // 2
        sent = lax.dynamic_slice_in_dim(block, (1 - upper) * length, length)
        kept = lax.dynamic_slice_in_dim(block, upper * length, length)
        block = kept + swapped(sent, "fsdp", step)
    return block


def group_sum(block):
    step = 0
    while 1 << step < lax.axis_size("fsdp"):
        block = block + swapped(block, "fsdp", step)
        step += 1
    return block


def core_rows(turned, core):
    chips = lax.axis_size("fsdp") // 2
    split = turned.reshape(chips, 2, -1, turned.shape[-1])
    picked = lax.dynamic_index_in_dim(split, core, 1, keepdims=False)
    return picked.reshape(-1, turned.shape[-1])


def chip_grad(left, right):
    core = lax.axis_index("fsdp") % 2
    turned = left.T
    mine = core_rows(turned, core)
    theirs = swapped(core_rows(turned, 1 - core), "fsdp", 0)
    rows = jnp.concatenate([mine, theirs], axis=1)
    grads = jnp.concatenate([right, swapped(right, "fsdp", 0)], axis=0)
    total = jnp.dot(rows, grads, preferred_element_type=jnp.float32)
    return total.reshape(lax.axis_size("fsdp") // 2, -1, right.shape[1])


def ring_sum(parts):
    chips, rows = parts.shape[:2]
    far = chips // 2
    cut = (rows // 2 + 7) // 8 * 8

    def part(apart):
        return lax.dynamic_index_in_dim(parts, chip_at(apart), 0, keepdims=False)

    def low(block):
        return block.astype(jnp.bfloat16)

    last = part(far)
    onward = hop(low(last[:cut]), 1)
    back = hop(low(last[cut:]), -1)
    for apart in range(far - 1, 0, -1):
        ahead, behind = part(apart), part(-apart)
        if apart == far - 1:
            ahead = jnp.concatenate([ahead[:cut] + onward, ahead[cut:]])
            behind = jnp.concatenate([behind[:cut], behind[cut:] + back])
        else:
            ahead, behind = ahead + onward, behind + back
        onward, back = hop(low(ahead), 1), hop(low(behind), -1)
    return part(0) + onward + back


def both_groups(block):
    rounded = lax.reduce_precision(block, 8, 7)
    return rounded + bins_peer(rounded.astype(jnp.bfloat16)).astype(jnp.float32)


def full_grad(left, right):
    return both_groups(ring_sum(chip_grad(left, right)))


def modulate(values, shift, scale):
    center = values - jnp.mean(values, axis=-1, keepdims=True)
    spread = jnp.mean(center * center, axis=-1, keepdims=True)
    return center * lax.rsqrt(spread + 1e-06) * (1.0 + scale) + shift


def cosine_sum(target_f, predicted):
    dots = jnp.sum(predicted * target_f, axis=-1)
    first = lax.rsqrt(jnp.sum(predicted * predicted, axis=-1) + 1e-06)
    second = lax.rsqrt(jnp.sum(target_f * target_f, axis=-1) + 1e-06)
    return jnp.sum(dots * first * second)


def product(left, right):
    return jnp.dot(left, right, preferred_element_type=jnp.float32)


def input_grad(grad, weight):
    return jnp.einsum("ne,de->nd", grad, weight, preferred_element_type=jnp.float32)


def shards(
    tokens,
    condition,
    segments,
    cotangent,
    target,
    w_ada,
    w_qkv,
    w_out,
    w_fc1,
    w_fc2,
    w_proj1,
    w_proj2,
    w_proj3,
):
    count = tokens.shape[0]
    width = tokens.shape[1]
    head_size = width // HEADS
    factor = head_size ** (-0.5)
    tokens_f = tokens.astype(jnp.float32)
    target_f = target.astype(jnp.float32)
    silu_cond, silu_back = jax.vjp(jax.nn.silu, condition)
    cond_low = silu_cond.astype(jnp.bfloat16)
    mod_cols = product(cond_low, w_ada)
    modulation = doubled(mod_cols.reshape(-1)).reshape(6, width)
    block_set = (
        lax.all_gather(w_qkv, "fsdp", axis=0, tiled=True),
        lax.all_gather(w_out, "fsdp", axis=0, tiled=True),
        lax.all_gather(w_fc1, "fsdp", axis=0, tiled=True),
        lax.all_gather(w_fc2, "fsdp", axis=0, tiled=True),
    )
    head_set = (
        lax.all_gather(w_proj1, "fsdp", axis=0, tiled=True),
        lax.all_gather(w_proj2, "fsdp", axis=0, tiled=True),
        lax.all_gather(w_proj3, "fsdp", axis=0, tiled=True),
    )
    full_qkv, full_out, full_fc1, full_fc2 = block_set
    head_first, head_second, head_third = head_set
    h_one, norm_one_back = jax.vjp(modulate, tokens_f, modulation[0], modulation[1])
    in_one = h_one.astype(jnp.bfloat16)
    qkv_low = product(in_one, full_qkv).astype(jnp.bfloat16).reshape(count, 3, HEADS, head_size)
    queries = qkv_low[:, 0]
    pair_own = jnp.stack([qkv_low[:, 1], qkv_low[:, 2]])
    pair_peer = swapped(pair_own, "fsdp", 0)
    keys_all = jnp.concatenate([pair_own[0], pair_peer[0]], axis=0)
    values_all = jnp.concatenate([pair_own[1], pair_peer[1]], axis=0)
    place = lax.axis_index("fsdp")
    own_ids = lax.dynamic_slice_in_dim(segments, place * count, count)
    peer_ids = lax.dynamic_slice_in_dim(segments, jnp.bitwise_xor(place, 1) * count, count)
    same = own_ids[:, None] == jnp.concatenate([own_ids, peer_ids])[None, :]
    raw = jnp.einsum("qhd,khd->hqk", queries, keys_all, preferred_element_type=jnp.float32) * factor
    masked = jnp.where(same[None], raw, -1e30)
    highest = jnp.max(masked, axis=-1, keepdims=True)
    expo = jnp.exp(masked - highest)
    totals = jnp.sum(expo, axis=-1, keepdims=True)
    log_total = highest + jnp.log(totals)
    probs_low = (expo / totals).astype(jnp.bfloat16)
    attended = jnp.einsum("hqk,khd->qhd", probs_low, values_all, preferred_element_type=jnp.float32)
    attended = attended.astype(jnp.bfloat16).reshape(count, width)
    branch_one = product(attended, full_out)
    resid_one = tokens_f + modulation[2] * branch_one
    h_two, norm_two_back = jax.vjp(modulate, resid_one, modulation[3], modulation[4])
    in_two = h_two.astype(jnp.bfloat16)
    hidden_pre = product(in_two, full_fc1)
    hidden_act, gelu_back = jax.vjp(partial(jax.nn.gelu, approximate=True), hidden_pre)
    hidden_low = hidden_act.astype(jnp.bfloat16)
    branch_two = product(hidden_low, full_fc2)
    result = resid_one + modulation[5] * branch_two
    result_low = result.astype(jnp.bfloat16)
    first_act, first_back = jax.vjp(jax.nn.silu, product(result_low, head_first))
    first_low = first_act.astype(jnp.bfloat16)
    second_act, second_back = jax.vjp(jax.nn.silu, product(first_low, head_second))
    second_low = second_act.astype(jnp.bfloat16)
    predicted = product(second_low, head_third)
    cos_total, cos_back = jax.vjp(partial(cosine_sum, target_f), predicted)
    (grad_pred,) = cos_back(jnp.float32(-1.0))
    grad_pred_low = grad_pred.astype(jnp.bfloat16)
    grad_third = full_grad(second_low, grad_pred_low)
    (grad_second_pre,) = second_back(input_grad(grad_pred_low, head_third))
    grad_second_low = grad_second_pre.astype(jnp.bfloat16)
    grad_second = full_grad(first_low, grad_second_low)
    (grad_first_pre,) = first_back(input_grad(grad_second_low, head_second))
    grad_first_low = grad_first_pre.astype(jnp.bfloat16)
    grad_first = full_grad(result_low, grad_first_low)
    d_result = cotangent.astype(jnp.float32) + input_grad(grad_first_low, head_first)
    grad_gate_two = jnp.sum(d_result * branch_two, axis=0)
    d_branch_two = (d_result * modulation[5]).astype(jnp.bfloat16)
    grad_fc2 = full_grad(hidden_low, d_branch_two)
    (d_pre,) = gelu_back(input_grad(d_branch_two, full_fc2))
    d_pre_low = d_pre.astype(jnp.bfloat16)
    grad_fc1 = full_grad(in_two, d_pre_low)
    d_resid_part, grad_shift_two, grad_scale_two = norm_two_back(input_grad(d_pre_low, full_fc1))
    d_resid = d_result + d_resid_part
    grad_gate_one = jnp.sum(d_resid * branch_one, axis=0)
    d_branch_one = (d_resid * modulation[2]).astype(jnp.bfloat16)
    grad_out = full_grad(attended, d_branch_one)
    d_attended = (
        input_grad(d_branch_one, full_out).astype(jnp.bfloat16).reshape(count, HEADS, head_size)
    )
    again_raw = (
        jnp.einsum("qhd,khd->hqk", queries, keys_all, preferred_element_type=jnp.float32) * factor
    )
    probs = jnp.exp(jnp.where(same[None], again_raw, -1e30) - log_total)
    probs_again = probs.astype(jnp.bfloat16)
    d_probs = jnp.einsum("qhd,khd->hqk", d_attended, values_all, preferred_element_type=jnp.float32)
    centre = jnp.sum(d_probs * probs, axis=-1, keepdims=True)
    d_scores = (probs * (d_probs - centre)).astype(jnp.bfloat16)
    d_queries = (
        jnp.einsum("hqk,khd->qhd", d_scores, keys_all, preferred_element_type=jnp.float32) * factor
    )
    d_keys = (
        jnp.einsum("hqk,qhd->khd", d_scores, queries, preferred_element_type=jnp.float32) * factor
    )
    d_values = jnp.einsum(
        "hqk,qhd->khd", probs_again, d_attended, preferred_element_type=jnp.float32
    )
    from_peer = swapped(jnp.stack([d_keys[count:], d_values[count:]]), "fsdp", 0)
    keys_grad = d_keys[:count] + from_peer[0]
    values_grad = d_values[:count] + from_peer[1]
    d_qkv = (
        jnp.stack([d_queries, keys_grad, values_grad], axis=1)
        .reshape(count, 3 * width)
        .astype(jnp.bfloat16)
    )
    grad_qkv = full_grad(in_one, d_qkv)
    d_tok_part, grad_shift_one, grad_scale_one = norm_one_back(input_grad(d_qkv, full_qkv))
    grad_tokens = d_resid + d_tok_part
    d_modulation = jnp.stack(
        [
            grad_shift_one,
            grad_scale_one,
            grad_gate_one,
            grad_shift_two,
            grad_scale_two,
            grad_gate_two,
        ]
    ).reshape(6 * width)
    mod_grad_cols = halved(d_modulation).reshape(1, -1)
    cond_part = jnp.dot(mod_grad_cols, w_ada.astype(jnp.float32).T, precision=HIGH)
    (grad_condition,) = silu_back(group_sum(cond_part))
    group = lax.axis_index("bins")
    cond_low_f = cond_low.astype(jnp.float32)
    other_cond, other_cols = bins_peer(cond_low_f), bins_peer(mod_grad_cols)
    first_cond = jnp.where(group == 0, cond_low_f, other_cond)
    last_cond = jnp.where(group == 0, other_cond, cond_low_f)
    first_cols = jnp.where(group == 0, mod_grad_cols, other_cols)
    last_cols = jnp.where(group == 0, other_cols, mod_grad_cols)
    grad_ada = first_cond.T * first_cols + last_cond.T * last_cols
    return (
        result_low,
        grad_tokens,
        grad_condition,
        grad_ada,
        grad_qkv,
        grad_out,
        grad_fc1,
        grad_fc2,
        grad_first,
        grad_second,
        grad_third,
    )


def solution(mesh):
    placed = (
        P(("bins", "fsdp"), None),
        P("bins", None),
        P("bins"),
        P(("bins", "fsdp"), None),
        P(("bins", "fsdp"), None),
        P(None, "fsdp"),
        P("fsdp", None),
        P("fsdp", None),
        P("fsdp", None),
        P("fsdp", None),
        P("fsdp", None),
        P("fsdp", None),
        P("fsdp", None),
    )
    return jax.shard_map(
        shards,
        mesh=mesh,
        in_specs=placed,
        out_specs=(
            P(("bins", "fsdp"), None),
            P(("bins", "fsdp"), None),
            P("bins", None),
            P(None, "fsdp"),
            P("fsdp", None),
            P("fsdp", None),
            P("fsdp", None),
            P("fsdp", None),
            P("fsdp", None),
            P("fsdp", None),
            P("fsdp", None),
        ),
        check_vma=False,
    )
```

```python
from functools import partial
from math import gcd

import jax
import jax.numpy as jnp
from jax import lax
from jax.experimental import pallas as pl
from jax.experimental.pallas import tpu as pltpu
from jax.sharding import PartitionSpec as P

HEADS = 16
SHORT = 256
HIGH = lax.Precision.HIGHEST
NT = (((1,), (1,)), ((), ()))
TN = (((0,), (0,)), ((), ()))
NN = (((1,), (0,)), ((), ()))


def mat(left, right, dims):
    return lax.dot_general(left, right, dims, preferred_element_type=jnp.float32)


def head_window(head, width):
    size = width // HEADS
    first = jnp.minimum(head * size // 128, width // 128 - 2) * 128
    lane = lax.broadcasted_iota(jnp.int32, (1, 256), 1)
    low = head * size - first
    return pl.multiple_of(first, 128), (lane >= low) & (lane < low + size)


def attend_kernel(factor, long_ref, q_ref, k_ref, v_ref, kp_ref, vp_ref, att_ref, exact_ref, turned_ref, log_ref, sums):
    count, width = q_ref.shape
    sums[...] = jnp.zeros_like(sums)

    def attend(head, key_parts, cols):
        first, mask = head_window(head, width)
        window = pl.ds(first, 256)
        queries = jnp.where(mask, q_ref[cols, window], 0)
        scores = [mat(k[rows, window], queries, NT) for k, v, rows in key_parts]
        highest = scores[0].max(axis=0, keepdims=True)
        for more in scores[1:]:
            highest = jnp.maximum(highest, more.max(axis=0, keepdims=True))
        expos = [jnp.exp((score - highest) * factor) for score in scores]
        total, out = 0.0, 0.0
        for expo in expos:
            total = total + expo.sum(axis=0, keepdims=True)
        share = 1.0 / total
        for (k, v, rows), expo in zip(key_parts, expos):
            values = jnp.where(mask, v[rows, window], 0)
            out = out + mat(values, (expo * share).astype(jnp.bfloat16), TN)
        sums[window, cols] += out
        log_ref[pl.ds(head, 1), cols] = highest * factor + jnp.log(total)

    everything = pl.ds(0, count)

    @pl.when(long_ref[0] == 1)
    def _():
        @pl.loop(0, HEADS, unroll=2)
        def _(head):
            attend(head, [(k_ref, v_ref, everything), (kp_ref, vp_ref, everything)], everything)

    @pl.when(long_ref[0] == 0)
    def _():
        @pl.loop(0, HEADS, unroll=2)
        def _(head):
            for top in range(0, count, SHORT):
                attend(head, [(k_ref, v_ref, pl.ds(top, SHORT))], pl.ds(top, SHORT))

    turned_ref[...] = sums[...].astype(jnp.bfloat16)
    exact_ref[...] = sums[...].T
    att_ref[...] = exact_ref[...].astype(jnp.bfloat16)


def part_spec(count, width, number):
    return pl.BlockSpec((count, width), lambda i: (0, number), pipeline_mode=pl.Buffered(1))


def attend(long, qkv, peer, factor):
    count, width = qkv.shape[0], qkv.shape[1] // 3
    flops = 4 * HEADS * count * 2 * count * 256
    return pl.pallas_call(
        partial(attend_kernel, factor),
        out_shape=[
            jax.ShapeDtypeStruct((count, width), jnp.bfloat16),
            jax.ShapeDtypeStruct((count, width), jnp.float32),
            jax.ShapeDtypeStruct((width, count), jnp.bfloat16),
            jax.ShapeDtypeStruct((HEADS, count), jnp.float32),
        ],
        grid=(1,),
        in_specs=[pl.BlockSpec(memory_space=pltpu.SMEM)]
        + [part_spec(count, width, j) for j in (0, 1, 2, 0, 1)],
        out_specs=[part_spec(count, width, 0)] * 2
        + [part_spec(width, count, 0), part_spec(HEADS, count, 0)],
        scratch_shapes=[pltpu.VMEM((width, count), jnp.float32)],
        compiler_params=pltpu.CompilerParams(vmem_limit_bytes=40 << 20),
        cost_estimate=pl.CostEstimate(flops=flops, transcendentals=HEADS * count * 2 * count, bytes_accessed=16 * count * width),
    )(long, qkv, qkv, qkv, peer, peer)


def attend_back_kernel(factor, long_ref, q_ref, k_ref, v_ref, kp_ref, vp_ref, grad_ref, exact_ref, log_ref, dq_ref, dk_ref, dv_ref, peer_ref, sums):
    count, width = q_ref.shape
    for ref in (sums, dk_ref, dv_ref, peer_ref):
        ref[...] = jnp.zeros_like(ref)

    def back(head, key_parts, cols):
        first, mask = head_window(head, width)
        window = pl.ds(first, 256)
        queries = jnp.where(mask, q_ref[cols, window], 0)
        grads = jnp.where(mask, grad_ref[cols, window], 0)
        weighed = grads.astype(jnp.float32) * exact_ref[cols, window]
        ones = jnp.ones((8, 256), jnp.float32)
        centre = lax.dot_general(ones, weighed, NT, precision=lax.Precision.HIGHEST, preferred_element_type=jnp.float32)[:1]
        logs = log_ref[pl.ds(head, 1), cols]
        turned = 0.0
        for k, v, rows, dk, dv, base in key_parts:
            keys = k[rows, window]
            probs = jnp.exp(mat(keys, queries, NT) * factor - logs)
            d_probs = mat(v[rows, window], grads, NT)
            d_scores = (probs * (d_probs - centre)).astype(jnp.bfloat16)
            spot = pl.ds(base + first, 256) if base else window
            dk[rows, window] += mat(d_scores, queries, NN) * factor
            dv[rows, spot] += mat(probs.astype(jnp.bfloat16), grads, NN)
            turned = turned + mat(jnp.where(mask, keys, 0), d_scores, TN)
        sums[window, cols] += turned * factor

    everything = pl.ds(0, count)

    @pl.when(long_ref[0] == 1)
    def _():
        @pl.loop(0, HEADS, unroll=2)
        def _(head):
            back(head, [(k_ref, v_ref, everything, dk_ref, dv_ref, 0), (kp_ref, vp_ref, everything, peer_ref, peer_ref, width)], everything)

    @pl.when(long_ref[0] == 0)
    def _():
        @pl.loop(0, HEADS, unroll=2)
        def _(head):
            for top in range(0, count, SHORT):
                back(head, [(k_ref, v_ref, pl.ds(top, SHORT), dk_ref, dv_ref, 0)], pl.ds(top, SHORT))

    dq_ref[...] = sums[...].T.astype(jnp.bfloat16)


def attend_back(long, qkv, peer, grad, exact, logs, factor):
    count, width = grad.shape
    flops = 10 * HEADS * count * 2 * count * 256
    full = part_spec(count, width, 0)
    return pl.pallas_call(
        partial(attend_back_kernel, factor),
        out_shape=[
            jax.ShapeDtypeStruct((count, width), jnp.bfloat16),
            jax.ShapeDtypeStruct((count, width), jnp.float32),
            jax.ShapeDtypeStruct((count, width), jnp.float32),
            jax.ShapeDtypeStruct((count, 2 * width), jnp.float32),
        ],
        grid=(1,),
        in_specs=[pl.BlockSpec(memory_space=pltpu.SMEM)]
        + [part_spec(count, width, j) for j in (0, 1, 2, 0, 1)]
        + [full, full, part_spec(HEADS, count, 0)],
        out_specs=[full, full, full, part_spec(count, 2 * width, 0)],
        scratch_shapes=[pltpu.VMEM((width, count), jnp.float32)],
        compiler_params=pltpu.CompilerParams(vmem_limit_bytes=48 << 20),
        cost_estimate=pl.CostEstimate(flops=flops, transcendentals=HEADS * count * 2 * count, bytes_accessed=40 * count * width),
    )(long, qkv, qkv, qkv, peer, peer, grad, exact, logs)


def swapped(block, axis, apart):
    count = lax.axis_size(axis)
    route = []
    for low in range(count):
        high = low | 1 << apart
        if high != low and high < count:
            route += [(low, high), (high, low)]
    return lax.ppermute(block, axis, route)


def bins_peer(block):
    return lax.ppermute(block, "bins", [(0, 1), (1, 0)])


def ring_route(chips):
    route = [2 * chip for chip in range(chips // 2)]
    return route + [chip + 1 for chip in reversed(route)]


def hop(block, apart):
    chips = lax.axis_size("fsdp") // 2
    route = ring_route(chips)
    pairs = []
    for spot, chip in enumerate(route):
        onward = route[(spot + apart) % chips]
        pairs += [(2 * chip, 2 * onward), (2 * chip + 1, 2 * onward + 1)]
    return lax.ppermute(block, "fsdp", pairs)


def parted_hop(block, apart):
    count, groups = lax.axis_size("fsdp"), lax.axis_size("bins")
    chips = count // 2
    route = ring_route(chips)
    pairs = []
    for group in range(groups):
        for spot, chip in enumerate(route):
            for core in range(2):
                way = apart if (group + core) % 2 == 0 else -apart
                onward = route[(spot + way) % chips]
                base = group * count + core
                pairs.append((base + 2 * chip, base + 2 * onward))
    return lax.ppermute(block, ("bins", "fsdp"), pairs)


def chip_at(apart):
    chips = lax.axis_size("fsdp") // 2
    chip = lax.axis_index("fsdp") // 2
    spot = jnp.where(chip % 2 == 0, chip // 2, chips - 1 - chip // 2)
    spot = (spot + apart) % chips
    return jnp.where(spot < chips // 2, 2 * spot, 2 * (chips - 1 - spot) + 1)


def gathered(block):
    core = lax.axis_index("fsdp") % 2
    parity = (lax.axis_index("bins") + core) % 2
    far = lax.axis_size("fsdp") // 4
    near = max(1, round(far / 3))
    half = block.shape[0] // 2
    ahead, behind, peers = [block], [block], {}
    fresh = [(0, block)]
    step = 0
    while fresh:
        step += 1
        flights = [(place, swapped(piece, "fsdp", 0), True) for place, piece in fresh]
        if step < far:
            flights.append((step, parted_hop(ahead[-1], 1), False))
        if step == far:
            part = lax.dynamic_slice_in_dim(ahead[-1], parity * half, half)
            flights.append((far, parted_hop(part, 1), False))
        if step <= near:
            flights.append((-step, parted_hop(behind[-1], -1), False))
        if near < step - 1 < far:
            flights.append((1 - step, bins_peer(ahead[step - 1]), False))
        if step == far + 1:
            flights.append((far, bins_peer(arm), False))
        arrived = yield [flight for _, flight, _ in flights]
        fresh = []
        for (place, _, swap), piece in zip(flights, arrived):
            if swap:
                peers[place] = piece
                continue
            if place == far and step == far:
                arm = piece
                continue
            if place == far:
                first = jnp.where(parity == 0, arm, piece)
                piece = jnp.concatenate([first, jnp.where(parity == 0, piece, arm)])
            (behind if place < 0 else ahead).append(piece)
            fresh.append((place, piece))
    way = 1 - 2 * parity
    places = [*range(far + 1), *(-place for place in range(1, far))]
    origins = [2 * chip_at(-way * place) + core for place in places]
    origins += [2 * chip_at(way * place) + 1 - core for place in places]
    pieces = ahead + behind[1:] + [peers[place] for place in places]
    return pieces, jnp.stack(origins).astype(jnp.int32)


def slabs(block):
    return block.reshape(-1, 8, block.shape[-1])


def assemble(pieces, origins, layout, shapes):
    width = pieces[0].shape[-1]
    copies = len(pieces) * len(layout)

    def kernel(origins_ref, *refs):
        blocks, wholes, sems = refs[: len(pieces)], refs[len(pieces) : -1], refs[-1]
        moves = []
        for number, block in enumerate(blocks):
            top = 0
            for weight, height, column in layout:
                spot = origins_ref[number] * height
                moves.append(
                    pltpu.make_async_copy(
                        block.at[pl.ds(top, height)],
                        wholes[weight].at[pl.ds(spot, height), :, pl.ds(column, width)],
                        sems.at[len(moves)],
                    )
                )
                top += height
        for move in moves:
            move.start()
        for move in moves:
            move.wait()

    size = 2 * sum(rows * columns for rows, columns in shapes)
    wholes = pl.pallas_call(
        kernel,
        out_shape=[jax.ShapeDtypeStruct((rows // 8, 8, columns), jnp.bfloat16) for rows, columns in shapes],
        in_specs=[pl.BlockSpec(memory_space=pltpu.SMEM)]
        + [pl.BlockSpec(memory_space=pl.ANY)] * len(pieces),
        out_specs=[pl.BlockSpec(memory_space=pltpu.VMEM)] * len(shapes),
        scratch_shapes=[pltpu.SemaphoreType.DMA((copies,))],
        compiler_params=pltpu.CompilerParams(vmem_limit_bytes=2 * size + (4 << 20)),
        cost_estimate=pl.CostEstimate(flops=0, transcendentals=0, bytes_accessed=2 * size),
    )(origins, *pieces)
    return [block.reshape(shape) for block, shape in zip(wholes, shapes)]


def whole(shards, width):
    if any(shard.shape[0] % 8 for shard in shards):
        return [lax.all_gather(shard, "fsdp", axis=0, tiled=True) for shard in shards]
    blocks, layout = [], []
    parts = max(shard.shape[1] // width for shard in shards)
    for column in range(parts):
        for weight, shard in enumerate(shards):
            if column * width < shard.shape[1]:
                blocks.append(shard[:, column * width : (column + 1) * width])
                layout.append((weight, shard.shape[0] // 8, column * width))
    block = jnp.concatenate([slabs(block) for block in blocks])
    count = lax.axis_size("fsdp")
    shapes = [(count * shard.shape[0], shard.shape[1]) for shard in shards]
    pieces, origins = yield from gathered(block)
    return assemble(pieces, origins, layout, shapes)


def doubled(block):
    count, place = lax.axis_size("fsdp"), lax.axis_index("fsdp")
    step = 0
    while 1 << step < count:
        other = yield swapped(block, "fsdp", step)
        upper = (place >> step) % 2 == 1
        block = jnp.where(
            upper, jnp.concatenate([other, block]), jnp.concatenate([block, other])
        )
        step += 1
    return block


def halved(block):
    count, place = lax.axis_size("fsdp"), lax.axis_index("fsdp")
    step = count.bit_length() - 1
    while step:
        step -= 1
        upper = (place >> step) % 2
        length = block.shape[0] // 2
        sent = lax.dynamic_slice_in_dim(block, (1 - upper) * length, length)
        kept = lax.dynamic_slice_in_dim(block, upper * length, length)
        block = kept + swapped(sent, "fsdp", step)
    return block


def group_sum(block):
    step = 0
    while 1 << step < lax.axis_size("fsdp"):
        block = block + swapped(block, "fsdp", step)
        step += 1
    return block


def core_rows(turned, core):
    chips = lax.axis_size("fsdp") // 2
    split = turned.reshape(chips, 2, -1, turned.shape[-1])
    picked = lax.dynamic_index_in_dim(split, core, 1, keepdims=False)
    return picked.reshape(-1, turned.shape[-1])


def chip_grad(left, right):
    core = lax.axis_index("fsdp") % 2
    turned = left.T
    mine = core_rows(turned, core)
    theirs = swapped(core_rows(turned, 1 - core), "fsdp", 0)
    rows = jnp.concatenate([mine, theirs], axis=1)
    grads = jnp.concatenate([right, swapped(right, "fsdp", 0)], axis=0)
    total = jnp.dot(rows, grads, preferred_element_type=jnp.float32)
    return total.reshape(lax.axis_size("fsdp") // 2, -1, right.shape[1])


def ring_sum(parts):
    chips, rows = parts.shape[:2]
    far = chips // 2
    cut = (rows // 2 + 7) // 8 * 8

    def part(apart):
        return lax.dynamic_index_in_dim(parts, chip_at(apart), 0, keepdims=False)

    def low(block):
        return block.astype(jnp.bfloat16)

    last = part(far)
    onward = hop(low(last[:cut]), 1)
    back = hop(low(last[cut:]), -1)
    for apart in range(far - 1, 0, -1):
        ahead, behind = part(apart), part(-apart)
        if apart == far - 1:
            ahead = jnp.concatenate([ahead[:cut] + onward, ahead[cut:]])
            behind = jnp.concatenate([behind[:cut], behind[cut:] + back])
        else:
            ahead, behind = ahead + onward, behind + back
        onward, back = hop(low(ahead), 1), hop(low(behind), -1)
    return part(0) + onward + back


def both_groups(block):
    rounded = lax.reduce_precision(block, 8, 7)
    return rounded + bins_peer(rounded.astype(jnp.bfloat16)).astype(jnp.float32)


def scattered_grad(left, right):
    total = jnp.einsum("nd,ne->de", left, right, preferred_element_type=jnp.float32)
    return lax.psum_scatter(total.astype(jnp.bfloat16), "fsdp", scatter_dimension=0, tiled=True)


def parts_kernel(spots_ref, mine_ref, theirs_ref, grad_ref, other_ref, *refs):
    outs, (turned, left, total) = refs[:-3], refs[-3:]
    number, half = len(outs), outs[0].shape[0]
    count, rows = mine_ref.shape[0], 2 * half

    @pl.when(pl.program_id(0) == 0)
    def _():
        for part in range(number):
            lanes = pl.ds(pl.multiple_of(spots_ref[0, part] * 128, 128), turned.shape[0])
            turned[:, :count] = mine_ref[:, lanes].T
            turned[:, count:] = theirs_ref[:, lanes].T
            low = pl.ds(pl.multiple_of(spots_ref[1, part], 16), rows)
            left[part * rows : (part + 1) * rows] = turned[low]

    total[...] = mat(left[:, :count], grad_ref[...], NN) + mat(left[:, count:], other_ref[...], NN)
    for part, out in enumerate(outs):
        first = part * rows
        if out.shape[0] == half:
            first = pl.multiple_of(first + spots_ref[2, 0] * half, 8)
        out[...] = total[pl.ds(first, out.shape[0]), :].astype(out.dtype)


def grad_parts(mine, theirs, grad, other, chips):
    (count, columns), features = grad.shape, mine.shape[1]
    rows = 2 * features // lax.axis_size("fsdp")
    reach = (rows + 128 - gcd(rows, 128) + 127) // 128 * 128
    starts = jnp.stack([jnp.asarray(chip, jnp.int32) * rows for chip in chips])
    windows = jnp.minimum(starts // 128, (features - reach) // 128)
    core = jnp.broadcast_to(lax.axis_index("fsdp") % 2, starts.shape)
    spots = jnp.stack([windows, starts - windows * 128, core.astype(jnp.int32)])
    tile, number = 1152 if columns > 2304 else 384, len(chips)
    if columns % tile:
        tile = 256
    tall = pl.BlockSpec((count, features), lambda i: (0, 0), pipeline_mode=pl.Buffered(1))
    wide = pl.BlockSpec((count, tile), lambda i: (0, i))
    kept = [rows // 2] + [rows] * (number - 2) + [rows // 2]
    kinds = [jnp.bfloat16] + [jnp.float32] * (number - 1)
    return pl.pallas_call(
        parts_kernel,
        out_shape=[jax.ShapeDtypeStruct((k, columns), kind) for k, kind in zip(kept, kinds)],
        grid=(columns // tile,),
        in_specs=[pl.BlockSpec(memory_space=pltpu.SMEM), tall, tall, wide, wide],
        out_specs=[pl.BlockSpec((k, tile), lambda i: (0, i)) for k in kept],
        scratch_shapes=[
            pltpu.VMEM((reach, 2 * count), jnp.bfloat16),
            pltpu.VMEM((number * rows, 2 * count), jnp.bfloat16),
            pltpu.VMEM((number * rows, tile), jnp.float32),
        ],
        compiler_params=pltpu.CompilerParams(vmem_limit_bytes=48 << 20),
        cost_estimate=pl.CostEstimate(
            flops=4 * number * rows * count * columns,
            transcendentals=0,
            bytes_accessed=4 * count * (columns + features) + 4 * (number - 1) * rows * columns,
        ),
    )(spots, mine, theirs, grad, other)


def core_hop(block):
    chips = lax.axis_size("fsdp") // 2
    route = ring_route(chips)
    pairs = []
    for spot, chip in enumerate(route):
        for core, way in ((0, 1), (1, -1)):
            pairs.append((2 * chip + core, 2 * route[(spot + way) % chips] + core))
    return lax.ppermute(block, "fsdp", pairs)


def grad_chain(left, right, theirs=None):
    rows = left.shape[1] // lax.axis_size("fsdp")
    if rows % 8:
        return full_grad(left, right)
    core = lax.axis_index("fsdp") % 2
    way = 1 - 2 * core
    far = lax.axis_size("fsdp") // 4
    if theirs is None:
        theirs = swapped(left, "fsdp", 0)
    other = yield swapped(right, "fsdp", 0)
    steps = list(range(far, 0, -1))
    chips = [chip_at(far)] + [chip_at(way * apart) for apart in steps[1:]] + [chip_at(0)]
    parts = grad_parts(left, theirs, right, other, chips)
    arrived = yield core_hop(parts[0])
    for number in range(1, far):
        if number == 1:
            first = jnp.where(core == 0, arrived, 0)
            arrived = jnp.concatenate([first, jnp.where(core == 0, 0, arrived)])
        arrived = yield core_hop((parts[number] + arrived).astype(jnp.bfloat16))
    kept = lax.dynamic_slice_in_dim(arrived, core * rows, rows)
    sent = lax.dynamic_slice_in_dim(arrived, (1 - core) * rows, rows)
    back = yield swapped(sent, "fsdp", 0)
    total = parts[far] + kept + back
    rounded = lax.reduce_precision(total, 8, 7)
    across = yield bins_peer(rounded.astype(jnp.bfloat16))
    return rounded + across.astype(jnp.float32)


class Chain:
    def __init__(self, steps):
        self.steps, self.flight, self.result = steps, (), None
        self.push(None)

    def push(self, arrived):
        if self.flight is None:
            return
        try:
            self.flight = self.steps.send(arrived)
        except StopIteration as stop:
            self.flight, self.result = None, stop.value

    def beat(self, *values):
        if self.flight is not None:
            values, arrived = lax.optimization_barrier((values, self.flight))
            self.push(arrived)
        return values if len(values) > 1 else values[0]

    def finish(self):
        while self.flight is not None:
            self.push(self.flight)
        return self.result


def full_grad(left, right):
    return both_groups(ring_sum(chip_grad(left, right)))


def modulate(values, shift, scale):
    center = values - jnp.mean(values, axis=-1, keepdims=True)
    spread = jnp.mean(center * center, axis=-1, keepdims=True)
    return center * lax.rsqrt(spread + 1e-06) * (1.0 + scale) + shift


def cosine_sum(target_f, predicted):
    dots = jnp.sum(predicted * target_f, axis=-1)
    first = lax.rsqrt(jnp.sum(predicted * predicted, axis=-1) + 1e-06)
    second = lax.rsqrt(jnp.sum(target_f * target_f, axis=-1) + 1e-06)
    return jnp.sum(dots * first * second)


def product(left, right):
    return jnp.dot(left, right, preferred_element_type=jnp.float32)


def input_grad(grad, weight):
    return jnp.einsum("ne,de->nd", grad, weight, preferred_element_type=jnp.float32)


def shards(
    tokens,
    condition,
    segments,
    cotangent,
    target,
    w_ada,
    w_qkv,
    w_out,
    w_fc1,
    w_fc2,
    w_proj1,
    w_proj2,
    w_proj3,
):
    count = tokens.shape[0]
    width = tokens.shape[1]
    head_size = width // HEADS
    factor = head_size ** (-0.5)
    tokens_f = tokens.astype(jnp.float32)
    target_f = target.astype(jnp.float32)
    silu_cond, silu_back = jax.vjp(jax.nn.silu, condition)
    cond_low = silu_cond.astype(jnp.bfloat16)
    mod_cols = product(cond_low, w_ada)
    first_set = Chain(whole([w_qkv, w_out], width))
    mod_chain = Chain(doubled(mod_cols.reshape(-1)))
    for _ in range(2):
        mod_chain.push(mod_chain.flight)
        first_set.push(first_set.flight)
    w_fc1, w_fc2, w_proj3 = first_set.beat(w_fc1, w_fc2, w_proj3)
    second_set = Chain(whole([w_fc1, w_fc2], width))
    head_third = lax.all_gather(w_proj3, "fsdp", axis=0, tiled=True)
    modulation = mod_chain.finish().reshape(6, width)
    full_qkv, full_out = first_set.finish()
    full_qkv, full_out = second_set.beat(full_qkv, full_out)
    h_one, norm_one_back = jax.vjp(modulate, tokens_f, modulation[0], modulation[1])
    in_one = h_one.astype(jnp.bfloat16)
    qkv_low = product(in_one, full_qkv).astype(jnp.bfloat16)
    peer_low = swapped(qkv_low[:, width:], "fsdp", 0)
    qkv_low, peer_low, w_proj1, w_proj2 = second_set.beat(qkv_low, peer_low, w_proj1, w_proj2)
    third_set = Chain(whole([w_proj1, w_proj2], w_proj1.shape[1] // 2))
    place = lax.axis_index("fsdp")
    own_ids = lax.dynamic_slice_in_dim(segments, place * count, count)
    long = (own_ids[:1] == own_ids[count - 1 :]).astype(jnp.int32)
    attended, exact, _, logs = attend(long, qkv_low, peer_low, factor)
    attended, exact, logs = second_set.beat(attended, exact, logs)
    attended, exact, logs = third_set.beat(attended, exact, logs)
    branch_one = product(attended, full_out)
    resid_one = tokens_f + modulation[2] * branch_one
    resid_one = second_set.beat(resid_one)
    resid_one = third_set.beat(resid_one)
    full_fc1, full_fc2 = second_set.finish()
    full_fc1, full_fc2 = third_set.beat(full_fc1, full_fc2)
    h_two, norm_two_back = jax.vjp(modulate, resid_one, modulation[3], modulation[4])
    in_two = h_two.astype(jnp.bfloat16)
    hidden_pre = product(in_two, full_fc1)
    hidden_act, gelu_back = jax.vjp(partial(jax.nn.gelu, approximate=True), hidden_pre)
    hidden_low = hidden_act.astype(jnp.bfloat16)
    hidden_low = third_set.beat(hidden_low)
    branch_two = product(hidden_low, full_fc2)
    result = resid_one + modulation[5] * branch_two
    result_low = result.astype(jnp.bfloat16)
    head_first, head_second = third_set.finish()
    first_act, first_back = jax.vjp(jax.nn.silu, product(result_low, head_first))
    first_low = first_act.astype(jnp.bfloat16)
    second_act, second_back = jax.vjp(jax.nn.silu, product(first_low, head_second))
    second_low = second_act.astype(jnp.bfloat16)
    predicted = product(second_low, head_third)
    cos_total, cos_back = jax.vjp(partial(cosine_sum, target_f), predicted)
    in_one_peer, in_two_peer, attended_peer, hidden_peer = (
        swapped(block, "fsdp", 0) for block in (in_one, in_two, attended, hidden_low)
    )
    (grad_pred,) = cos_back(jnp.float32(-1.0))
    grad_pred_low = grad_pred.astype(jnp.bfloat16)
    grad_third = scattered_grad(second_low, grad_pred_low)
    (grad_second_pre,) = second_back(input_grad(grad_pred_low, head_third))
    grad_second_low = grad_second_pre.astype(jnp.bfloat16)
    grad_second = scattered_grad(first_low, grad_second_low)
    (grad_first_pre,) = first_back(input_grad(grad_second_low, head_second))
    grad_first_low = grad_first_pre.astype(jnp.bfloat16)
    grad_first = scattered_grad(result_low, grad_first_low)
    d_result = cotangent.astype(jnp.float32) + input_grad(grad_first_low, head_first)
    grad_gate_two = jnp.sum(d_result * branch_two, axis=0)
    d_branch_two = (d_result * modulation[5]).astype(jnp.bfloat16)
    chain_fc2 = Chain(grad_chain(hidden_low, d_branch_two, hidden_peer))
    d_branch_two = chain_fc2.beat(d_branch_two)
    (d_pre,) = gelu_back(input_grad(d_branch_two, full_fc2))
    d_pre_low = d_pre.astype(jnp.bfloat16)
    d_pre_low = chain_fc2.beat(d_pre_low)
    chain_fc1 = Chain(grad_chain(in_two, d_pre_low, in_two_peer))
    d_resid_part, grad_shift_two, grad_scale_two = norm_two_back(input_grad(d_pre_low, full_fc1))
    d_resid_part = chain_fc1.beat(chain_fc2.beat(d_resid_part))
    d_resid = d_result + d_resid_part
    grad_gate_one = jnp.sum(d_resid * branch_one, axis=0)
    d_branch_one = (d_resid * modulation[2]).astype(jnp.bfloat16)
    chain_out = Chain(grad_chain(attended, d_branch_one, attended_peer))
    d_branch_one = chain_fc1.beat(d_branch_one)
    d_attended = input_grad(d_branch_one, full_out).astype(jnp.bfloat16)
    d_attended = chain_out.beat(chain_fc2.beat(d_attended))
    d_queries, d_keys, d_values, d_peer = attend_back(
        long, qkv_low, peer_low, d_attended, exact, logs, factor
    )
    from_peer = swapped(d_peer, "fsdp", 0)
    d_queries = chain_out.beat(chain_fc1.beat(d_queries))
    from_peer = chain_fc2.beat(from_peer)
    d_qkv = jnp.concatenate(
        [
            d_queries,
            (d_keys + from_peer[:, :width]).astype(jnp.bfloat16),
            (d_values + from_peer[:, width:]).astype(jnp.bfloat16),
        ],
        axis=1,
    )
    chain_qkv = Chain(grad_chain(in_one, d_qkv, in_one_peer))
    d_qkv = chain_out.beat(chain_fc1.beat(d_qkv))
    d_tok_part, grad_shift_one, grad_scale_one = norm_one_back(input_grad(d_qkv, full_qkv))
    d_tok_part = chain_qkv.beat(chain_fc1.beat(d_tok_part))
    d_tok_part, head_parts = lax.optimization_barrier(
        (d_tok_part, (grad_first, grad_second, grad_third))
    )
    grad_first, grad_second, grad_third = (
        both_groups(part.astype(jnp.float32)) for part in head_parts
    )
    grad_tokens = d_resid + d_tok_part
    grad_fc2, grad_out = chain_fc2.finish(), chain_out.finish()
    grad_fc1, grad_qkv = chain_fc1.finish(), chain_qkv.finish()
    d_modulation = jnp.stack(
        [
            grad_shift_one,
            grad_scale_one,
            grad_gate_one,
            grad_shift_two,
            grad_scale_two,
            grad_gate_two,
        ]
    ).reshape(6 * width)
    mod_grad_cols = halved(d_modulation).reshape(1, -1)
    cond_part = jnp.dot(mod_grad_cols, w_ada.astype(jnp.float32).T, precision=HIGH)
    (grad_condition,) = silu_back(group_sum(cond_part))
    group = lax.axis_index("bins")
    cond_low_f = cond_low.astype(jnp.float32)
    other_cond, other_cols = bins_peer(cond_low_f), bins_peer(mod_grad_cols)
    first_cond = jnp.where(group == 0, cond_low_f, other_cond)
    last_cond = jnp.where(group == 0, other_cond, cond_low_f)
    first_cols = jnp.where(group == 0, mod_grad_cols, other_cols)
    last_cols = jnp.where(group == 0, other_cols, mod_grad_cols)
    grad_ada = first_cond.T * first_cols + last_cond.T * last_cols
    return (
        result_low,
        grad_tokens,
        grad_condition,
        grad_ada,
        grad_qkv,
        grad_out,
        grad_fc1,
        grad_fc2,
        grad_first,
        grad_second,
        grad_third,
    )


def solution(mesh):
    placed = (
        P(("bins", "fsdp"), None),
        P("bins", None),
        P("bins"),
        P(("bins", "fsdp"), None),
        P(("bins", "fsdp"), None),
        P(None, "fsdp"),
        P("fsdp", None),
        P("fsdp", None),
        P("fsdp", None),
        P("fsdp", None),
        P("fsdp", None),
        P("fsdp", None),
        P("fsdp", None),
    )
    return jax.shard_map(
        shards,
        mesh=mesh,
        in_specs=placed,
        out_specs=(
            P(("bins", "fsdp"), None),
            P(("bins", "fsdp"), None),
            P("bins", None),
            P(None, "fsdp"),
            P("fsdp", None),
            P("fsdp", None),
            P("fsdp", None),
            P("fsdp", None),
            P("fsdp", None),
            P("fsdp", None),
            P("fsdp", None),
        ),
        check_vma=False,
    )
```

```python
from functools import partial
from math import gcd

import jax
import jax.numpy as jnp
from jax import lax
from jax.experimental import pallas as pl
from jax.experimental.pallas import tpu as pltpu
from jax.sharding import PartitionSpec as P

HEADS = 16
SHORT = 256
HIGH = lax.Precision.HIGHEST
NT = (((1,), (1,)), ((), ()))
TN = (((0,), (0,)), ((), ()))
NN = (((1,), (0,)), ((), ()))


def mat(left, right, dims):
    return lax.dot_general(left, right, dims, preferred_element_type=jnp.float32)


def head_window(head, width):
    size = width // HEADS
    first = jnp.minimum(head * size // 128, width // 128 - 2) * 128
    lane = lax.broadcasted_iota(jnp.int32, (1, 256), 1)
    low = head * size - first
    return pl.multiple_of(first, 128), (lane >= low) & (lane < low + size)


def attend_kernel(factor, long_ref, q_ref, k_ref, v_ref, kp_ref, vp_ref, att_ref, exact_ref, turned_ref, log_ref, sums):
    count, width = q_ref.shape
    sums[...] = jnp.zeros_like(sums)

    def attend(head, key_parts, cols):
        first, mask = head_window(head, width)
        window = pl.ds(first, 256)
        queries = jnp.where(mask, q_ref[cols, window], 0)
        scores = [mat(k[rows, window], queries, NT) for k, v, rows in key_parts]
        highest = scores[0].max(axis=0, keepdims=True)
        for more in scores[1:]:
            highest = jnp.maximum(highest, more.max(axis=0, keepdims=True))
        expos = [jnp.exp((score - highest) * factor) for score in scores]
        total, out = 0.0, 0.0
        for expo in expos:
            total = total + expo.sum(axis=0, keepdims=True)
        share = 1.0 / total
        for (k, v, rows), expo in zip(key_parts, expos):
            values = jnp.where(mask, v[rows, window], 0)
            out = out + mat(values, (expo * share).astype(jnp.bfloat16), TN)
        sums[window, cols] += out
        log_ref[pl.ds(head, 1), cols] = highest * factor + jnp.log(total)

    everything = pl.ds(0, count)

    @pl.when(long_ref[0] == 1)
    def _():
        @pl.loop(0, HEADS, unroll=2)
        def _(head):
            attend(head, [(k_ref, v_ref, everything), (kp_ref, vp_ref, everything)], everything)

    @pl.when(long_ref[0] == 0)
    def _():
        @pl.loop(0, HEADS, unroll=2)
        def _(head):
            for top in range(0, count, SHORT):
                attend(head, [(k_ref, v_ref, pl.ds(top, SHORT))], pl.ds(top, SHORT))

    turned_ref[...] = sums[...].astype(jnp.bfloat16)
    exact_ref[...] = sums[...].T
    att_ref[...] = exact_ref[...].astype(jnp.bfloat16)


def part_spec(count, width, number):
    return pl.BlockSpec((count, width), lambda i: (0, number), pipeline_mode=pl.Buffered(1))


def attend(long, qkv, peer, factor):
    count, width = qkv.shape[0], qkv.shape[1] // 3
    flops = 4 * HEADS * count * 2 * count * 256
    return pl.pallas_call(
        partial(attend_kernel, factor),
        out_shape=[
            jax.ShapeDtypeStruct((count, width), jnp.bfloat16),
            jax.ShapeDtypeStruct((count, width), jnp.float32),
            jax.ShapeDtypeStruct((width, count), jnp.bfloat16),
            jax.ShapeDtypeStruct((HEADS, count), jnp.float32),
        ],
        grid=(1,),
        in_specs=[pl.BlockSpec(memory_space=pltpu.SMEM)]
        + [part_spec(count, width, j) for j in (0, 1, 2, 0, 1)],
        out_specs=[part_spec(count, width, 0)] * 2
        + [part_spec(width, count, 0), part_spec(HEADS, count, 0)],
        scratch_shapes=[pltpu.VMEM((width, count), jnp.float32)],
        compiler_params=pltpu.CompilerParams(vmem_limit_bytes=40 << 20),
        cost_estimate=pl.CostEstimate(flops=flops, transcendentals=HEADS * count * 2 * count, bytes_accessed=16 * count * width),
    )(long, qkv, qkv, qkv, peer, peer)


def attend_back_kernel(factor, long_ref, q_ref, k_ref, v_ref, kp_ref, vp_ref, grad_ref, exact_ref, log_ref, dq_ref, dk_ref, dv_ref, peer_ref, sums):
    count, width = q_ref.shape
    for ref in (sums, dk_ref, dv_ref, peer_ref):
        ref[...] = jnp.zeros_like(ref)

    def back(head, key_parts, cols):
        first, mask = head_window(head, width)
        window = pl.ds(first, 256)
        queries = jnp.where(mask, q_ref[cols, window], 0)
        grads = jnp.where(mask, grad_ref[cols, window], 0)
        weighed = grads.astype(jnp.float32) * exact_ref[cols, window]
        ones = jnp.ones((8, 256), jnp.float32)
        centre = lax.dot_general(ones, weighed, NT, precision=lax.Precision.HIGHEST, preferred_element_type=jnp.float32)[:1]
        logs = log_ref[pl.ds(head, 1), cols]
        turned = 0.0
        for k, v, rows, dk, dv, base in key_parts:
            keys = k[rows, window]
            probs = jnp.exp(mat(keys, queries, NT) * factor - logs)
            d_probs = mat(v[rows, window], grads, NT)
            d_scores = (probs * (d_probs - centre)).astype(jnp.bfloat16)
            spot = pl.ds(base + first, 256) if base else window
            dk[rows, window] += mat(d_scores, queries, NN) * factor
            dv[rows, spot] += mat(probs.astype(jnp.bfloat16), grads, NN)
            turned = turned + mat(jnp.where(mask, keys, 0), d_scores, TN)
        sums[window, cols] += turned * factor

    everything = pl.ds(0, count)

    @pl.when(long_ref[0] == 1)
    def _():
        @pl.loop(0, HEADS, unroll=2)
        def _(head):
            back(head, [(k_ref, v_ref, everything, dk_ref, dv_ref, 0), (kp_ref, vp_ref, everything, peer_ref, peer_ref, width)], everything)

    @pl.when(long_ref[0] == 0)
    def _():
        @pl.loop(0, HEADS, unroll=2)
        def _(head):
            for top in range(0, count, SHORT):
                back(head, [(k_ref, v_ref, pl.ds(top, SHORT), dk_ref, dv_ref, 0)], pl.ds(top, SHORT))

    dq_ref[...] = sums[...].T.astype(jnp.bfloat16)


def attend_back(long, qkv, peer, grad, exact, logs, factor):
    count, width = grad.shape
    flops = 10 * HEADS * count * 2 * count * 256
    full = part_spec(count, width, 0)
    return pl.pallas_call(
        partial(attend_back_kernel, factor),
        out_shape=[
            jax.ShapeDtypeStruct((count, width), jnp.bfloat16),
            jax.ShapeDtypeStruct((count, width), jnp.float32),
            jax.ShapeDtypeStruct((count, width), jnp.float32),
            jax.ShapeDtypeStruct((count, 2 * width), jnp.float32),
        ],
        grid=(1,),
        in_specs=[pl.BlockSpec(memory_space=pltpu.SMEM)]
        + [part_spec(count, width, j) for j in (0, 1, 2, 0, 1)]
        + [full, full, part_spec(HEADS, count, 0)],
        out_specs=[full, full, full, part_spec(count, 2 * width, 0)],
        scratch_shapes=[pltpu.VMEM((width, count), jnp.float32)],
        compiler_params=pltpu.CompilerParams(vmem_limit_bytes=48 << 20),
        cost_estimate=pl.CostEstimate(flops=flops, transcendentals=HEADS * count * 2 * count, bytes_accessed=40 * count * width),
    )(long, qkv, qkv, qkv, peer, peer, grad, exact, logs)


def swapped(block, axis, apart):
    count = lax.axis_size(axis)
    route = []
    for low in range(count):
        high = low | 1 << apart
        if high != low and high < count:
            route += [(low, high), (high, low)]
    return lax.ppermute(block, axis, route)


def bins_peer(block):
    return lax.ppermute(block, "bins", [(0, 1), (1, 0)])


def ring_route(chips):
    route = [2 * chip for chip in range(chips // 2)]
    return route + [chip + 1 for chip in reversed(route)]


def hop(block, apart):
    chips = lax.axis_size("fsdp") // 2
    route = ring_route(chips)
    pairs = []
    for spot, chip in enumerate(route):
        onward = route[(spot + apart) % chips]
        pairs += [(2 * chip, 2 * onward), (2 * chip + 1, 2 * onward + 1)]
    return lax.ppermute(block, "fsdp", pairs)


def parted_hop(block, apart):
    count, groups = lax.axis_size("fsdp"), lax.axis_size("bins")
    chips = count // 2
    route = ring_route(chips)
    pairs = []
    for group in range(groups):
        for spot, chip in enumerate(route):
            for core in range(2):
                way = apart if (group + core) % 2 == 0 else -apart
                onward = route[(spot + way) % chips]
                base = group * count + core
                pairs.append((base + 2 * chip, base + 2 * onward))
    return lax.ppermute(block, ("bins", "fsdp"), pairs)


def chip_at(apart):
    chips = lax.axis_size("fsdp") // 2
    chip = lax.axis_index("fsdp") // 2
    spot = jnp.where(chip % 2 == 0, chip // 2, chips - 1 - chip // 2)
    spot = (spot + apart) % chips
    return jnp.where(spot < chips // 2, 2 * spot, 2 * (chips - 1 - spot) + 1)


def onward(block):
    return parted_hop(block, 1)


def backward(block):
    return parted_hop(block, -1)


def core_swap(block):
    return swapped(block, "fsdp", 0)


def each(sends):
    return lambda blocks: [send(block) for send, block in zip(sends, blocks)]


def gathered(block):
    core = lax.axis_index("fsdp") % 2
    parity = (lax.axis_index("bins") + core) % 2
    far = lax.axis_size("fsdp") // 4
    near = max(1, round(far / 3))
    half = block.shape[0] // 2
    ahead, behind, peers = [block], [block], {}
    fresh = [(0, block)]
    step = 0
    while fresh:
        step += 1
        flights = []
        if step < far:
            flights.append((step, onward, ahead[-1], False))
        if step == far:
            part = lax.dynamic_slice_in_dim(ahead[-1], parity * half, half)
            flights.append((far, onward, part, False))
        if step <= near:
            flights.append((-step, backward, behind[-1], False))
        if near < step - 1 < far:
            flights.append((1 - step, bins_peer, ahead[step - 1], False))
        if step == far + 1:
            flights.append((far, bins_peer, arm, False))
        flights += [(place, core_swap, piece, True) for place, piece in fresh]
        sends = [send for _, send, _, _ in flights]
        arrived = yield each(sends), [piece for _, _, piece, _ in flights]
        fresh = []
        for (place, _, _, swap), piece in zip(flights, arrived):
            if swap:
                peers[place] = piece
                continue
            if place == far and step == far:
                arm = piece
                continue
            if place == far:
                first = jnp.where(parity == 0, arm, piece)
                piece = jnp.concatenate([first, jnp.where(parity == 0, piece, arm)])
            (behind if place < 0 else ahead).append(piece)
            fresh.append((place, piece))
    way = 1 - 2 * parity
    places = [*range(far + 1), *(-place for place in range(1, far))]
    origins = [2 * chip_at(-way * place) + core for place in places]
    origins += [2 * chip_at(way * place) + 1 - core for place in places]
    pieces = ahead + behind[1:] + [peers[place] for place in places]
    return pieces, jnp.stack(origins).astype(jnp.int32)


def slabs(block):
    return block.reshape(-1, 8, block.shape[-1])


def assemble(pieces, origins, layout, shapes):
    width = pieces[0].shape[-1]
    copies = len(pieces) * len(layout)

    def kernel(origins_ref, *refs):
        blocks, wholes, sems = refs[: len(pieces)], refs[len(pieces) : -1], refs[-1]
        moves = []
        for number, block in enumerate(blocks):
            top = 0
            for weight, height, column in layout:
                spot = origins_ref[number] * height
                moves.append(
                    pltpu.make_async_copy(
                        block.at[pl.ds(top, height)],
                        wholes[weight].at[pl.ds(spot, height), :, pl.ds(column, width)],
                        sems.at[len(moves)],
                    )
                )
                top += height
        for move in moves:
            move.start()
        for move in moves:
            move.wait()

    size = 2 * sum(rows * columns for rows, columns in shapes)
    wholes = pl.pallas_call(
        kernel,
        out_shape=[jax.ShapeDtypeStruct((rows // 8, 8, columns), jnp.bfloat16) for rows, columns in shapes],
        in_specs=[pl.BlockSpec(memory_space=pltpu.SMEM)]
        + [pl.BlockSpec(memory_space=pl.ANY)] * len(pieces),
        out_specs=[pl.BlockSpec(memory_space=pltpu.VMEM)] * len(shapes),
        scratch_shapes=[pltpu.SemaphoreType.DMA((copies,))],
        compiler_params=pltpu.CompilerParams(vmem_limit_bytes=2 * size + (4 << 20)),
        cost_estimate=pl.CostEstimate(flops=0, transcendentals=0, bytes_accessed=2 * size),
    )(origins, *pieces)
    return [block.reshape(shape) for block, shape in zip(wholes, shapes)]


def whole(shards, width):
    if any(shard.shape[0] % 8 for shard in shards):
        return [lax.all_gather(shard, "fsdp", axis=0, tiled=True) for shard in shards]
    blocks, layout = [], []
    parts = max(shard.shape[1] // width for shard in shards)
    for column in range(parts):
        for weight, shard in enumerate(shards):
            if column * width < shard.shape[1]:
                blocks.append(shard[:, column * width : (column + 1) * width])
                layout.append((weight, shard.shape[0] // 8, column * width))
    block = jnp.concatenate([slabs(block) for block in blocks])
    count = lax.axis_size("fsdp")
    shapes = [(count * shard.shape[0], shard.shape[1]) for shard in shards]
    pieces, origins = yield from gathered(block)
    return assemble(pieces, origins, layout, shapes)


def doubled(block):
    count, place = lax.axis_size("fsdp"), lax.axis_index("fsdp")
    step = 0
    while 1 << step < count:
        other = yield partial(swapped, axis="fsdp", apart=step), block
        upper = (place >> step) % 2 == 1
        block = jnp.where(
            upper, jnp.concatenate([other, block]), jnp.concatenate([block, other])
        )
        step += 1
    return block


def column_sums(block, columns_weight):
    count, place = lax.axis_size("fsdp"), lax.axis_index("fsdp")
    step = count.bit_length() - 1
    while step:
        step -= 1
        upper = (place >> step) % 2
        length = block.shape[0] // 2
        sent = lax.dynamic_slice_in_dim(block, (1 - upper) * length, length)
        kept = lax.dynamic_slice_in_dim(block, upper * length, length)
        block = kept + (yield partial(swapped, axis="fsdp", apart=step), sent)
    columns = block.reshape(1, -1)
    total = jnp.dot(columns, columns_weight.astype(jnp.float32).T, precision=HIGH)
    across = yield bins_peer, columns
    while 1 << step < count:
        total = total + (yield partial(swapped, axis="fsdp", apart=step), total)
        step += 1
    return columns, across, total


def core_rows(turned, core):
    chips = lax.axis_size("fsdp") // 2
    split = turned.reshape(chips, 2, -1, turned.shape[-1])
    picked = lax.dynamic_index_in_dim(split, core, 1, keepdims=False)
    return picked.reshape(-1, turned.shape[-1])


def chip_grad(left, right):
    core = lax.axis_index("fsdp") % 2
    turned = left.T
    mine = core_rows(turned, core)
    theirs = swapped(core_rows(turned, 1 - core), "fsdp", 0)
    rows = jnp.concatenate([mine, theirs], axis=1)
    grads = jnp.concatenate([right, swapped(right, "fsdp", 0)], axis=0)
    total = jnp.dot(rows, grads, preferred_element_type=jnp.float32)
    return total.reshape(lax.axis_size("fsdp") // 2, -1, right.shape[1])


def ring_sum(parts):
    chips, rows = parts.shape[:2]
    far = chips // 2
    cut = (rows // 2 + 7) // 8 * 8

    def part(apart):
        return lax.dynamic_index_in_dim(parts, chip_at(apart), 0, keepdims=False)

    def low(block):
        return block.astype(jnp.bfloat16)

    last = part(far)
    onward = hop(low(last[:cut]), 1)
    back = hop(low(last[cut:]), -1)
    for apart in range(far - 1, 0, -1):
        ahead, behind = part(apart), part(-apart)
        if apart == far - 1:
            ahead = jnp.concatenate([ahead[:cut] + onward, ahead[cut:]])
            behind = jnp.concatenate([behind[:cut], behind[cut:] + back])
        else:
            ahead, behind = ahead + onward, behind + back
        onward, back = hop(low(ahead), 1), hop(low(behind), -1)
    return part(0) + onward + back


def both_groups(block):
    rounded = lax.reduce_precision(block, 8, 7)
    return rounded + bins_peer(rounded.astype(jnp.bfloat16)).astype(jnp.float32)


def scattered(block):
    return lax.psum_scatter(block, "fsdp", scatter_dimension=0, tiled=True)


def low_grad(left, right):
    total = jnp.einsum("nd,ne->de", left, right, preferred_element_type=jnp.float32)
    return total.astype(jnp.bfloat16)


def parts_kernel(spots_ref, mine_ref, theirs_ref, grad_ref, other_ref, *refs):
    outs, (turned, left, total) = refs[:-3], refs[-3:]
    number, half = len(outs), outs[0].shape[0]
    count, rows = mine_ref.shape[0], 2 * half

    @pl.when(pl.program_id(0) == 0)
    def _():
        for part in range(number):
            lanes = pl.ds(pl.multiple_of(spots_ref[0, part] * 128, 128), turned.shape[0])
            turned[:, :count] = mine_ref[:, lanes].T
            turned[:, count:] = theirs_ref[:, lanes].T
            low = pl.ds(pl.multiple_of(spots_ref[1, part], 16), rows)
            left[part * rows : (part + 1) * rows] = turned[low]

    total[...] = mat(left[:, :count], grad_ref[...], NN) + mat(left[:, count:], other_ref[...], NN)
    for part, out in enumerate(outs):
        first = part * rows
        if out.shape[0] == half:
            first = pl.multiple_of(first + spots_ref[2, 0] * half, 8)
        out[...] = total[pl.ds(first, out.shape[0]), :].astype(out.dtype)


def grad_parts(mine, theirs, grad, other, chips):
    (count, columns), features = grad.shape, mine.shape[1]
    rows = 2 * features // lax.axis_size("fsdp")
    reach = (rows + 128 - gcd(rows, 128) + 127) // 128 * 128
    starts = jnp.stack([jnp.asarray(chip, jnp.int32) * rows for chip in chips])
    windows = jnp.minimum(starts // 128, (features - reach) // 128)
    core = jnp.broadcast_to(lax.axis_index("fsdp") % 2, starts.shape)
    spots = jnp.stack([windows, starts - windows * 128, core.astype(jnp.int32)])
    tile, number = 1152 if columns > 2304 else 384, len(chips)
    if columns % tile:
        tile = 256
    tall = pl.BlockSpec((count, features), lambda i: (0, 0), pipeline_mode=pl.Buffered(1))
    wide = pl.BlockSpec((count, tile), lambda i: (0, i))
    kept = [rows // 2] + [rows] * (number - 2) + [rows // 2]
    kinds = [jnp.bfloat16] + [jnp.float32] * (number - 1)
    return pl.pallas_call(
        parts_kernel,
        out_shape=[jax.ShapeDtypeStruct((k, columns), kind) for k, kind in zip(kept, kinds)],
        grid=(columns // tile,),
        in_specs=[pl.BlockSpec(memory_space=pltpu.SMEM), tall, tall, wide, wide],
        out_specs=[pl.BlockSpec((k, tile), lambda i: (0, i)) for k in kept],
        scratch_shapes=[
            pltpu.VMEM((reach, 2 * count), jnp.bfloat16),
            pltpu.VMEM((number * rows, 2 * count), jnp.bfloat16),
            pltpu.VMEM((number * rows, tile), jnp.float32),
        ],
        compiler_params=pltpu.CompilerParams(vmem_limit_bytes=48 << 20),
        cost_estimate=pl.CostEstimate(
            flops=4 * number * rows * count * columns,
            transcendentals=0,
            bytes_accessed=4 * count * (columns + features) + 4 * (number - 1) * rows * columns,
        ),
    )(spots, mine, theirs, grad, other)


def core_hop(block):
    chips = lax.axis_size("fsdp") // 2
    route = ring_route(chips)
    pairs = []
    for spot, chip in enumerate(route):
        for core, way in ((0, 1), (1, -1)):
            pairs.append((2 * chip + core, 2 * route[(spot + way) % chips] + core))
    return lax.ppermute(block, "fsdp", pairs)


def bins_sum(part):
    across = yield bins_peer, part
    return part.astype(jnp.float32) + across.astype(jnp.float32)


def grad_chain(pairs, theirs):
    heights = [left.shape[1] // lax.axis_size("fsdp") for left, _ in pairs]
    if any(rows % 8 for rows in heights):
        return [full_grad(left, right) for left, right in pairs]
    core = lax.axis_index("fsdp") % 2
    way = 1 - 2 * core
    far = lax.axis_size("fsdp") // 4
    others = yield each([core_swap] * len(pairs)), [right for _, right in pairs]
    steps = list(range(far, 0, -1))
    chips = [chip_at(far)] + [chip_at(way * apart) for apart in steps[1:]] + [chip_at(0)]
    parts = [
        grad_parts(left, peer, right, other, chips)
        for (left, right), peer, other in zip(pairs, theirs, others)
    ]

    def joined(blocks):
        return blocks[0] if len(blocks) == 1 else jnp.concatenate(blocks)

    def split(block, times):
        out, top = [], 0
        for rows in heights:
            out.append(block[top : top + times * rows])
            top += times * rows
        return out

    arrived = yield core_hop, joined([part[0] for part in parts])
    for number in range(1, far):
        if number == 1:
            spread = []
            for half in split(arrived, 1):
                spread += [jnp.where(core == 0, half, 0), jnp.where(core == 0, 0, half)]
            arrived = jnp.concatenate(spread)
        sums = [part[number] + block for part, block in zip(parts, split(arrived, 2))]
        arrived = yield core_hop, joined([block.astype(jnp.bfloat16) for block in sums])
    kept = [lax.dynamic_slice_in_dim(block, core * rows, rows) for block, rows in zip(split(arrived, 2), heights)]
    sent = [lax.dynamic_slice_in_dim(block, (1 - core) * rows, rows) for block, rows in zip(split(arrived, 2), heights)]
    back = yield core_swap, joined(sent)
    rounded = [
        lax.reduce_precision(part[far] + mine + more, 8, 7)
        for part, mine, more in zip(parts, kept, split(back, 1))
    ]
    across = yield bins_peer, joined([block.astype(jnp.bfloat16) for block in rounded])
    return [block + more.astype(jnp.float32) for block, more in zip(rounded, split(across, 1))]


class Chain:
    def __init__(self, steps):
        self.steps, self.flight, self.result = steps, (), None
        self.take(None)
        self.launch()

    def take(self, arrived):
        try:
            self.send, self.block = self.steps.send(arrived)
        except StopIteration as stop:
            self.send, self.block, self.result = None, None, stop.value

    def launch(self):
        self.flight = None if self.send is None else self.send(self.block)

    def push(self):
        if self.flight is not None:
            self.take(self.flight)
            self.launch()

    def finish(self):
        while self.flight is not None:
            self.push()
        return self.result


def arrive(values, *chains):
    chains = [chain for chain in chains if chain.flight is not None]
    if not chains:
        return values
    values, flights = lax.optimization_barrier((values, [chain.flight for chain in chains]))
    for chain, flight in zip(chains, flights):
        chain.take(flight)
    return values


def depart(values, *chains):
    ready = [(chain.block, chain.result) for chain in chains]
    values, ready = lax.optimization_barrier((values, ready))
    for chain, (chain.block, chain.result) in zip(chains, ready):
        chain.launch()
    return values


def beats(values, *chains):
    chains = [chain for chain in chains if chain.flight is not None]
    return depart(arrive(values, *chains), *chains) if chains else values


def full_grad(left, right):
    return both_groups(ring_sum(chip_grad(left, right)))


def modulate(values, shift, scale):
    center = values - jnp.mean(values, axis=-1, keepdims=True)
    spread = jnp.mean(center * center, axis=-1, keepdims=True)
    return center * lax.rsqrt(spread + 1e-06) * (1.0 + scale) + shift


def cosine_sum(target_f, predicted):
    dots = jnp.sum(predicted * target_f, axis=-1)
    first = lax.rsqrt(jnp.sum(predicted * predicted, axis=-1) + 1e-06)
    second = lax.rsqrt(jnp.sum(target_f * target_f, axis=-1) + 1e-06)
    return jnp.sum(dots * first * second)


def product(left, right):
    return jnp.dot(left, right, preferred_element_type=jnp.float32)


def input_grad(grad, weight):
    return jnp.einsum("ne,de->nd", grad, weight, preferred_element_type=jnp.float32)


def shards(
    tokens,
    condition,
    segments,
    cotangent,
    target,
    w_ada,
    w_qkv,
    w_out,
    w_fc1,
    w_fc2,
    w_proj1,
    w_proj2,
    w_proj3,
):
    count = tokens.shape[0]
    width = tokens.shape[1]
    head_size = width // HEADS
    factor = head_size ** (-0.5)
    tokens_f = tokens.astype(jnp.float32)
    target_f = target.astype(jnp.float32)
    silu_cond, silu_back = jax.vjp(jax.nn.silu, condition)
    cond_low = silu_cond.astype(jnp.bfloat16)
    mod_cols = product(cond_low, w_ada)
    first_set = Chain(whole([w_qkv, w_out], width))
    mod_chain = Chain(doubled(mod_cols.reshape(-1)))
    for _ in range(2):
        first_set.push()
        mod_chain.push()
    w_fc1, w_fc2, w_proj3 = beats((w_fc1, w_fc2, w_proj3), first_set)
    second_set = Chain(whole([w_fc1, w_fc2], width))
    head_third = lax.all_gather(w_proj3, "fsdp", axis=0, tiled=True)
    modulation = mod_chain.finish().reshape(6, width)
    full_qkv, full_out = first_set.finish()
    full_qkv, full_out = beats((full_qkv, full_out), second_set)
    h_one, norm_one_back = jax.vjp(modulate, tokens_f, modulation[0], modulation[1])
    in_one = h_one.astype(jnp.bfloat16)
    qkv_low = product(in_one, full_qkv).astype(jnp.bfloat16)
    peer_low = swapped(qkv_low[:, width:], "fsdp", 0)
    qkv_low, peer_low, w_proj1, w_proj2 = beats(
        (qkv_low, peer_low, w_proj1, w_proj2), second_set
    )
    third_set = Chain(whole([w_proj1, w_proj2], w_proj1.shape[1] // 2))
    place = lax.axis_index("fsdp")
    own_ids = lax.dynamic_slice_in_dim(segments, place * count, count)
    long = (own_ids[:1] == own_ids[count - 1 :]).astype(jnp.int32)
    attended, exact, _, logs = attend(long, qkv_low, peer_low, factor)
    attended, exact, logs = beats((attended, exact, logs), second_set)
    attended, exact, logs = beats((attended, exact, logs), third_set)
    branch_one = product(attended, full_out)
    resid_one = tokens_f + modulation[2] * branch_one
    resid_one = beats(resid_one, second_set)
    resid_one = beats(resid_one, third_set)
    full_fc1, full_fc2 = second_set.finish()
    full_fc1, full_fc2 = beats((full_fc1, full_fc2), third_set)
    h_two, norm_two_back = jax.vjp(modulate, resid_one, modulation[3], modulation[4])
    in_two = h_two.astype(jnp.bfloat16)
    hidden_pre = product(in_two, full_fc1)
    hidden_act, gelu_back = jax.vjp(partial(jax.nn.gelu, approximate=True), hidden_pre)
    hidden_low = hidden_act.astype(jnp.bfloat16)
    hidden_low = beats(hidden_low, third_set)
    branch_two = product(hidden_low, full_fc2)
    result = resid_one + modulation[5] * branch_two
    result_low = result.astype(jnp.bfloat16)
    head_first, head_second = third_set.finish()
    first_act, first_back = jax.vjp(jax.nn.silu, product(result_low, head_first))
    first_low = first_act.astype(jnp.bfloat16)
    second_act, second_back = jax.vjp(jax.nn.silu, product(first_low, head_second))
    second_low = second_act.astype(jnp.bfloat16)
    predicted = product(second_low, head_third)
    cos_total, cos_back = jax.vjp(partial(cosine_sum, target_f), predicted)
    in_one_peer, in_two_peer, attended_peer, hidden_peer = (
        swapped(block, "fsdp", 0) for block in (in_one, in_two, attended, hidden_low)
    )
    (grad_pred,) = cos_back(jnp.float32(-1.0))
    grad_pred_low = grad_pred.astype(jnp.bfloat16)
    total_third = low_grad(second_low, grad_pred_low)
    grad_pred_low, total_third = lax.optimization_barrier((grad_pred_low, total_third))
    part_third = scattered(total_third)
    (grad_second_pre,) = second_back(input_grad(grad_pred_low, head_third))
    grad_second_low = grad_second_pre.astype(jnp.bfloat16)
    total_second = low_grad(first_low, grad_second_low)
    grad_second_low, total_second = lax.optimization_barrier((grad_second_low, total_second))
    part_second = scattered(total_second)
    (grad_first_pre,) = first_back(input_grad(grad_second_low, head_second))
    grad_first_low = grad_first_pre.astype(jnp.bfloat16)
    d_result = cotangent.astype(jnp.float32) + input_grad(grad_first_low, head_first)
    total_first = low_grad(result_low, grad_first_low)
    d_result, total_first = lax.optimization_barrier((d_result, total_first))
    part_first = scattered(total_first)
    grad_gate_two = jnp.sum(d_result * branch_two, axis=0)
    d_branch_two = (d_result * modulation[5]).astype(jnp.bfloat16)
    chain_fc2 = Chain(grad_chain([(hidden_low, d_branch_two)], [hidden_peer]))
    (d_pre,) = gelu_back(input_grad(d_branch_two, full_fc2))
    d_pre_low = d_pre.astype(jnp.bfloat16)
    d_pre_low = beats(d_pre_low, chain_fc2)
    d_pre_low, part_third = lax.optimization_barrier((d_pre_low, part_third))
    chain_third = Chain(bins_sum(part_third))
    chain_fc1 = Chain(grad_chain([(in_two, d_pre_low)], [in_two_peer]))
    d_in_two = input_grad(d_pre_low, full_fc1)
    d_resid_part, grad_shift_two, grad_scale_two = norm_two_back(d_in_two)
    d_resid = d_result + d_resid_part
    grad_gate_one = jnp.sum(d_resid * branch_one, axis=0)
    d_branch_one = (d_resid * modulation[2]).astype(jnp.bfloat16)
    d_branch_one, d_resid = beats((d_branch_one, d_resid), chain_fc2)
    chain_out = Chain(grad_chain([(attended, d_branch_one)], [attended_peer]))
    d_branch_one = beats(d_branch_one, chain_fc1)
    d_attended = input_grad(d_branch_one, full_out).astype(jnp.bfloat16)
    d_attended = beats(d_attended, chain_out)
    d_attended = beats(d_attended, chain_fc2, chain_third)
    busy = [chain for chain in (chain_fc2, chain_fc1) if chain.flight is not None]
    d_queries, d_keys, d_values, d_peer = arrive(
        attend_back(long, qkv_low, peer_low, d_attended, exact, logs, factor), *busy
    )
    from_peer = swapped(d_peer, "fsdp", 0)
    d_queries = depart(d_queries, *busy)
    d_qkv = jnp.concatenate(
        [
            d_queries,
            (d_keys + from_peer[:, :width]).astype(jnp.bfloat16),
            (d_values + from_peer[:, width:]).astype(jnp.bfloat16),
        ],
        axis=1,
    )
    chain_qkv = Chain(grad_chain([(in_one, d_qkv)], [in_one_peer]))
    d_in_one = input_grad(d_qkv, full_qkv)
    d_in_one = beats(d_in_one, chain_qkv)
    d_in_one, part_second = lax.optimization_barrier((d_in_one, part_second))
    chain_second = Chain(bins_sum(part_second))
    d_tok_part, grad_shift_one, grad_scale_one = norm_one_back(d_in_one)
    d_modulation = jnp.stack(
        [
            grad_shift_one,
            grad_scale_one,
            grad_gate_one,
            grad_shift_two,
            grad_scale_two,
            grad_gate_two,
        ]
    ).reshape(6 * width)
    grad_tokens = d_resid + d_tok_part
    chain_mod = Chain(column_sums(d_modulation, w_ada))
    rounds = (
        (chain_fc2, chain_fc1, chain_out, chain_mod),
        (chain_qkv, chain_fc2, chain_mod, chain_second),
        (chain_fc1, chain_out, chain_mod),
        (chain_qkv, chain_mod),
        (chain_fc1, chain_out, chain_fc2, chain_mod),
        (chain_qkv, chain_fc1, chain_out, chain_mod),
    )
    for number, chains in enumerate(rounds):
        grad_tokens = beats(grad_tokens, *chains)
        if number == 2:
            grad_tokens, part_first = lax.optimization_barrier((grad_tokens, part_first))
            chain_first = Chain(bins_sum(part_first))
    grad_tokens = beats(grad_tokens, chain_qkv, chain_first, chain_mod)
    grad_tokens = beats(grad_tokens, chain_qkv, chain_fc1, chain_out, chain_mod)
    grad_first, grad_second, grad_third = (
        chain.finish() for chain in (chain_first, chain_second, chain_third)
    )
    mod_grad_cols, other_cols, cond_total = chain_mod.finish()
    (grad_qkv,), (grad_fc1,), (grad_out,), (grad_fc2,) = (
        chain.finish() for chain in (chain_qkv, chain_fc1, chain_out, chain_fc2)
    )
    (grad_condition,) = silu_back(cond_total)
    group = lax.axis_index("bins")
    cond_low_f = cond_low.astype(jnp.float32)
    other_cond = bins_peer(cond_low_f)
    first_cond = jnp.where(group == 0, cond_low_f, other_cond)
    last_cond = jnp.where(group == 0, other_cond, cond_low_f)
    first_cols = jnp.where(group == 0, mod_grad_cols, other_cols)
    last_cols = jnp.where(group == 0, other_cols, mod_grad_cols)
    grad_ada = first_cond.T * first_cols + last_cond.T * last_cols
    return (
        result_low,
        grad_tokens,
        grad_condition,
        grad_ada,
        grad_qkv,
        grad_out,
        grad_fc1,
        grad_fc2,
        grad_first,
        grad_second,
        grad_third,
    )


def solution(mesh):
    placed = (
        P(("bins", "fsdp"), None),
        P("bins", None),
        P("bins"),
        P(("bins", "fsdp"), None),
        P(("bins", "fsdp"), None),
        P(None, "fsdp"),
        P("fsdp", None),
        P("fsdp", None),
        P("fsdp", None),
        P("fsdp", None),
        P("fsdp", None),
        P("fsdp", None),
        P("fsdp", None),
    )
    return jax.shard_map(
        shards,
        mesh=mesh,
        in_specs=placed,
        out_specs=(
            P(("bins", "fsdp"), None),
            P(("bins", "fsdp"), None),
            P("bins", None),
            P(None, "fsdp"),
            P("fsdp", None),
            P("fsdp", None),
            P("fsdp", None),
            P("fsdp", None),
            P("fsdp", None),
            P("fsdp", None),
            P("fsdp", None),
        ),
        check_vma=False,
    )
```

```python
from functools import partial
from math import gcd

import jax
import jax.numpy as jnp
from jax import lax
from jax.experimental import pallas as pl
from jax.experimental.pallas import tpu as pltpu
from jax.sharding import PartitionSpec as P

HEADS = 16
SHORT = 256
HIGH = lax.Precision.HIGHEST
NT = (((1,), (1,)), ((), ()))
TN = (((0,), (0,)), ((), ()))
NN = (((1,), (0,)), ((), ()))


def mat(left, right, dims):
    return lax.dot_general(left, right, dims, preferred_element_type=jnp.float32)


def head_window(head, width):
    size = width // HEADS
    first = jnp.minimum(head * size // 128, width // 128 - 2) * 128
    lane = lax.broadcasted_iota(jnp.int32, (1, 256), 1)
    low = head * size - first
    return pl.multiple_of(first, 128), (lane >= low) & (lane < low + size)


def attend_kernel(factor, long_ref, q_ref, k_ref, v_ref, kp_ref, vp_ref, att_ref, exact_ref, turned_ref, log_ref, sums):
    count, width = q_ref.shape
    sums[...] = jnp.zeros_like(sums)

    def attend(head, key_parts, cols):
        first, mask = head_window(head, width)
        window = pl.ds(first, 256)
        queries = jnp.where(mask, q_ref[cols, window], 0)
        scores = [mat(k[rows, window], queries, NT) for k, v, rows in key_parts]
        highest = scores[0].max(axis=0, keepdims=True)
        for more in scores[1:]:
            highest = jnp.maximum(highest, more.max(axis=0, keepdims=True))
        expos = [jnp.exp((score - highest) * factor) for score in scores]
        total, out = 0.0, 0.0
        for expo in expos:
            total = total + expo.sum(axis=0, keepdims=True)
        share = 1.0 / total
        for (k, v, rows), expo in zip(key_parts, expos):
            values = jnp.where(mask, v[rows, window], 0)
            out = out + mat(values, (expo * share).astype(jnp.bfloat16), TN)
        sums[window, cols] += out
        log_ref[pl.ds(head, 1), cols] = highest * factor + jnp.log(total)

    everything = pl.ds(0, count)

    @pl.when(long_ref[0] == 1)
    def _():
        @pl.loop(0, HEADS, unroll=2)
        def _(head):
            attend(head, [(k_ref, v_ref, everything), (kp_ref, vp_ref, everything)], everything)

    @pl.when(long_ref[0] == 0)
    def _():
        @pl.loop(0, HEADS, unroll=2)
        def _(head):
            for top in range(0, count, SHORT):
                attend(head, [(k_ref, v_ref, pl.ds(top, SHORT))], pl.ds(top, SHORT))

    turned_ref[...] = sums[...].astype(jnp.bfloat16)
    exact_ref[...] = sums[...].T
    att_ref[...] = exact_ref[...].astype(jnp.bfloat16)


def part_spec(count, width, number):
    return pl.BlockSpec((count, width), lambda i: (0, number), pipeline_mode=pl.Buffered(1))


def attend(long, qkv, peer, factor):
    count, width = qkv.shape[0], qkv.shape[1] // 3
    flops = 4 * HEADS * count * 2 * count * 256
    return pl.pallas_call(
        partial(attend_kernel, factor),
        out_shape=[
            jax.ShapeDtypeStruct((count, width), jnp.bfloat16),
            jax.ShapeDtypeStruct((count, width), jnp.float32),
            jax.ShapeDtypeStruct((width, count), jnp.bfloat16),
            jax.ShapeDtypeStruct((HEADS, count), jnp.float32),
        ],
        grid=(1,),
        in_specs=[pl.BlockSpec(memory_space=pltpu.SMEM)]
        + [part_spec(count, width, j) for j in (0, 1, 2, 0, 1)],
        out_specs=[part_spec(count, width, 0)] * 2
        + [part_spec(width, count, 0), part_spec(HEADS, count, 0)],
        scratch_shapes=[pltpu.VMEM((width, count), jnp.float32)],
        compiler_params=pltpu.CompilerParams(vmem_limit_bytes=40 << 20),
        cost_estimate=pl.CostEstimate(flops=flops, transcendentals=HEADS * count * 2 * count, bytes_accessed=16 * count * width),
    )(long, qkv, qkv, qkv, peer, peer)


def attend_back_kernel(factor, long_ref, q_ref, k_ref, v_ref, kp_ref, vp_ref, grad_ref, exact_ref, log_ref, dq_ref, dk_ref, dv_ref, peer_ref, sums):
    count, width = q_ref.shape
    for ref in (sums, dk_ref, dv_ref, peer_ref):
        ref[...] = jnp.zeros_like(ref)

    def back(head, key_parts, cols):
        first, mask = head_window(head, width)
        window = pl.ds(first, 256)
        queries = jnp.where(mask, q_ref[cols, window], 0)
        grads = jnp.where(mask, grad_ref[cols, window], 0)
        weighed = grads.astype(jnp.float32) * exact_ref[cols, window]
        ones = jnp.ones((8, 256), jnp.float32)
        centre = lax.dot_general(ones, weighed, NT, precision=lax.Precision.HIGHEST, preferred_element_type=jnp.float32)[:1]
        logs = log_ref[pl.ds(head, 1), cols]
        turned = 0.0
        for k, v, rows, dk, dv, base in key_parts:
            keys = k[rows, window]
            probs = jnp.exp(mat(keys, queries, NT) * factor - logs)
            d_probs = mat(v[rows, window], grads, NT)
            d_scores = (probs * (d_probs - centre)).astype(jnp.bfloat16)
            spot = pl.ds(base + first, 256) if base else window
            dk[rows, window] += mat(d_scores, queries, NN) * factor
            dv[rows, spot] += mat(probs.astype(jnp.bfloat16), grads, NN)
            turned = turned + mat(jnp.where(mask, keys, 0), d_scores, TN)
        sums[window, cols] += turned * factor

    everything = pl.ds(0, count)

    @pl.when(long_ref[0] == 1)
    def _():
        @pl.loop(0, HEADS, unroll=2)
        def _(head):
            back(head, [(k_ref, v_ref, everything, dk_ref, dv_ref, 0), (kp_ref, vp_ref, everything, peer_ref, peer_ref, width)], everything)

    @pl.when(long_ref[0] == 0)
    def _():
        @pl.loop(0, HEADS, unroll=2)
        def _(head):
            for top in range(0, count, SHORT):
                back(head, [(k_ref, v_ref, pl.ds(top, SHORT), dk_ref, dv_ref, 0)], pl.ds(top, SHORT))

    dq_ref[...] = sums[...].T.astype(jnp.bfloat16)


def attend_back(long, qkv, peer, grad, exact, logs, factor):
    count, width = grad.shape
    flops = 10 * HEADS * count * 2 * count * 256
    full = part_spec(count, width, 0)
    return pl.pallas_call(
        partial(attend_back_kernel, factor),
        out_shape=[
            jax.ShapeDtypeStruct((count, width), jnp.bfloat16),
            jax.ShapeDtypeStruct((count, width), jnp.float32),
            jax.ShapeDtypeStruct((count, width), jnp.float32),
            jax.ShapeDtypeStruct((count, 2 * width), jnp.float32),
        ],
        grid=(1,),
        in_specs=[pl.BlockSpec(memory_space=pltpu.SMEM)]
        + [part_spec(count, width, j) for j in (0, 1, 2, 0, 1)]
        + [full, full, part_spec(HEADS, count, 0)],
        out_specs=[full, full, full, part_spec(count, 2 * width, 0)],
        scratch_shapes=[pltpu.VMEM((width, count), jnp.float32)],
        compiler_params=pltpu.CompilerParams(vmem_limit_bytes=48 << 20),
        cost_estimate=pl.CostEstimate(flops=flops, transcendentals=HEADS * count * 2 * count, bytes_accessed=40 * count * width),
    )(long, qkv, qkv, qkv, peer, peer, grad, exact, logs)


def swapped(block, axis, apart):
    count = lax.axis_size(axis)
    route = []
    for low in range(count):
        high = low | 1 << apart
        if high != low and high < count:
            route += [(low, high), (high, low)]
    return lax.ppermute(block, axis, route)


def bins_peer(block):
    return lax.ppermute(block, "bins", [(0, 1), (1, 0)])


def ring_route(chips):
    route = [2 * chip for chip in range(chips // 2)]
    return route + [chip + 1 for chip in reversed(route)]


def hop(block, apart):
    chips = lax.axis_size("fsdp") // 2
    route = ring_route(chips)
    pairs = []
    for spot, chip in enumerate(route):
        onward = route[(spot + apart) % chips]
        pairs += [(2 * chip, 2 * onward), (2 * chip + 1, 2 * onward + 1)]
    return lax.ppermute(block, "fsdp", pairs)


def parted_hop(block, apart):
    count, groups = lax.axis_size("fsdp"), lax.axis_size("bins")
    chips = count // 2
    route = ring_route(chips)
    pairs = []
    for group in range(groups):
        for spot, chip in enumerate(route):
            for core in range(2):
                way = apart if (group + core) % 2 == 0 else -apart
                onward = route[(spot + way) % chips]
                base = group * count + core
                pairs.append((base + 2 * chip, base + 2 * onward))
    return lax.ppermute(block, ("bins", "fsdp"), pairs)


def chip_at(apart):
    chips = lax.axis_size("fsdp") // 2
    chip = lax.axis_index("fsdp") // 2
    spot = jnp.where(chip % 2 == 0, chip // 2, chips - 1 - chip // 2)
    spot = (spot + apart) % chips
    return jnp.where(spot < chips // 2, 2 * spot, 2 * (chips - 1 - spot) + 1)


def onward(block):
    return parted_hop(block, 1)


def backward(block):
    return parted_hop(block, -1)


def core_swap(block):
    return swapped(block, "fsdp", 0)


def each(sends):
    return lambda blocks: [send(block) for send, block in zip(sends, blocks)]


def gathered(block):
    core = lax.axis_index("fsdp") % 2
    parity = (lax.axis_index("bins") + core) % 2
    far = lax.axis_size("fsdp") // 4
    near = max(1, round(far / 3))
    half = block.shape[0] // 2
    ahead, behind, peers = [block], [block], {}
    fresh = [(0, block)]
    step = 0
    while fresh:
        step += 1
        flights = []
        if step < far:
            flights.append((step, onward, ahead[-1], False))
        if step == far:
            part = lax.dynamic_slice_in_dim(ahead[-1], parity * half, half)
            flights.append((far, onward, part, False))
        if step <= near:
            flights.append((-step, backward, behind[-1], False))
        if near < step - 1 < far:
            flights.append((1 - step, bins_peer, ahead[step - 1], False))
        if step == far + 1:
            flights.append((far, bins_peer, arm, False))
        flights += [(place, core_swap, piece, True) for place, piece in fresh]
        sends = [send for _, send, _, _ in flights]
        arrived = yield each(sends), [piece for _, _, piece, _ in flights]
        fresh = []
        for (place, _, _, swap), piece in zip(flights, arrived):
            if swap:
                peers[place] = piece
                continue
            if place == far and step == far:
                arm = piece
                continue
            if place == far:
                first = jnp.where(parity == 0, arm, piece)
                piece = jnp.concatenate([first, jnp.where(parity == 0, piece, arm)])
            (behind if place < 0 else ahead).append(piece)
            fresh.append((place, piece))
    way = 1 - 2 * parity
    places = [*range(far + 1), *(-place for place in range(1, far))]
    origins = [2 * chip_at(-way * place) + core for place in places]
    origins += [2 * chip_at(way * place) + 1 - core for place in places]
    pieces = ahead + behind[1:] + [peers[place] for place in places]
    return pieces, jnp.stack(origins).astype(jnp.int32)


def slabs(block):
    return block.reshape(-1, 8, block.shape[-1])


def assemble(pieces, origins, layout, shapes):
    width = pieces[0].shape[-1]
    copies = len(pieces) * len(layout)

    def kernel(origins_ref, *refs):
        blocks, wholes, sems = refs[: len(pieces)], refs[len(pieces) : -1], refs[-1]
        moves = []
        for number, block in enumerate(blocks):
            top = 0
            for weight, height, column in layout:
                spot = origins_ref[number] * height
                moves.append(
                    pltpu.make_async_copy(
                        block.at[pl.ds(top, height)],
                        wholes[weight].at[pl.ds(spot, height), :, pl.ds(column, width)],
                        sems.at[len(moves)],
                    )
                )
                top += height
        for move in moves:
            move.start()
        for move in moves:
            move.wait()

    size = 2 * sum(rows * columns for rows, columns in shapes)
    wholes = pl.pallas_call(
        kernel,
        out_shape=[jax.ShapeDtypeStruct((rows // 8, 8, columns), jnp.bfloat16) for rows, columns in shapes],
        in_specs=[pl.BlockSpec(memory_space=pltpu.SMEM)]
        + [pl.BlockSpec(memory_space=pl.ANY)] * len(pieces),
        out_specs=[pl.BlockSpec(memory_space=pltpu.VMEM)] * len(shapes),
        scratch_shapes=[pltpu.SemaphoreType.DMA((copies,))],
        compiler_params=pltpu.CompilerParams(vmem_limit_bytes=2 * size + (4 << 20)),
        cost_estimate=pl.CostEstimate(flops=0, transcendentals=0, bytes_accessed=2 * size),
    )(origins, *pieces)
    return [block.reshape(shape) for block, shape in zip(wholes, shapes)]


def whole(shards, width):
    if any(shard.shape[0] % 8 for shard in shards):
        return [lax.all_gather(shard, "fsdp", axis=0, tiled=True) for shard in shards]
    blocks, layout = [], []
    parts = max(shard.shape[1] // width for shard in shards)
    for column in range(parts):
        for weight, shard in enumerate(shards):
            if column * width < shard.shape[1]:
                blocks.append(shard[:, column * width : (column + 1) * width])
                layout.append((weight, shard.shape[0] // 8, column * width))
    block = jnp.concatenate([slabs(block) for block in blocks])
    count = lax.axis_size("fsdp")
    shapes = [(count * shard.shape[0], shard.shape[1]) for shard in shards]
    pieces, origins = yield from gathered(block)
    return assemble(pieces, origins, layout, shapes)


def doubled(block):
    count, place = lax.axis_size("fsdp"), lax.axis_index("fsdp")
    step = 0
    while 1 << step < count:
        other = yield partial(swapped, axis="fsdp", apart=step), block
        upper = (place >> step) % 2 == 1
        block = jnp.where(
            upper, jnp.concatenate([other, block]), jnp.concatenate([block, other])
        )
        step += 1
    return block


def column_sums(block, columns_weight):
    count, place = lax.axis_size("fsdp"), lax.axis_index("fsdp")
    step = count.bit_length() - 1
    while step:
        step -= 1
        upper = (place >> step) % 2
        length = block.shape[0] // 2
        sent = lax.dynamic_slice_in_dim(block, (1 - upper) * length, length)
        kept = lax.dynamic_slice_in_dim(block, upper * length, length)
        block = kept + (yield partial(swapped, axis="fsdp", apart=step), sent)
    columns = block.reshape(1, -1)
    total = jnp.dot(columns, columns_weight.astype(jnp.float32).T, precision=HIGH)
    across = yield bins_peer, columns
    while 1 << step < count:
        total = total + (yield partial(swapped, axis="fsdp", apart=step), total)
        step += 1
    return columns, across, total


def core_rows(turned, core):
    chips = lax.axis_size("fsdp") // 2
    split = turned.reshape(chips, 2, -1, turned.shape[-1])
    picked = lax.dynamic_index_in_dim(split, core, 1, keepdims=False)
    return picked.reshape(-1, turned.shape[-1])


def chip_grad(left, right):
    core = lax.axis_index("fsdp") % 2
    turned = left.T
    mine = core_rows(turned, core)
    theirs = swapped(core_rows(turned, 1 - core), "fsdp", 0)
    rows = jnp.concatenate([mine, theirs], axis=1)
    grads = jnp.concatenate([right, swapped(right, "fsdp", 0)], axis=0)
    total = jnp.dot(rows, grads, preferred_element_type=jnp.float32)
    return total.reshape(lax.axis_size("fsdp") // 2, -1, right.shape[1])


def ring_sum(parts):
    chips, rows = parts.shape[:2]
    far = chips // 2
    cut = (rows // 2 + 7) // 8 * 8

    def part(apart):
        return lax.dynamic_index_in_dim(parts, chip_at(apart), 0, keepdims=False)

    def low(block):
        return block.astype(jnp.bfloat16)

    last = part(far)
    onward = hop(low(last[:cut]), 1)
    back = hop(low(last[cut:]), -1)
    for apart in range(far - 1, 0, -1):
        ahead, behind = part(apart), part(-apart)
        if apart == far - 1:
            ahead = jnp.concatenate([ahead[:cut] + onward, ahead[cut:]])
            behind = jnp.concatenate([behind[:cut], behind[cut:] + back])
        else:
            ahead, behind = ahead + onward, behind + back
        onward, back = hop(low(ahead), 1), hop(low(behind), -1)
    return part(0) + onward + back


def both_groups(block):
    rounded = lax.reduce_precision(block, 8, 7)
    return rounded + bins_peer(rounded.astype(jnp.bfloat16)).astype(jnp.float32)


def scattered(block):
    return lax.psum_scatter(block, "fsdp", scatter_dimension=0, tiled=True)


def low_grad(left, right):
    total = jnp.einsum("nd,ne->de", left, right, preferred_element_type=jnp.float32)
    return total.astype(jnp.bfloat16)


def parts_kernel(spots_ref, mine_ref, theirs_ref, grad_ref, other_ref, *refs):
    outs, (turned, left, total) = refs[:-3], refs[-3:]
    number, half = len(outs), outs[0].shape[0]
    count, rows = mine_ref.shape[0], 2 * half

    @pl.when(pl.program_id(0) == 0)
    def _():
        for part in range(number):
            lanes = pl.ds(pl.multiple_of(spots_ref[0, part] * 128, 128), turned.shape[0])
            turned[:, :count] = mine_ref[:, lanes].T
            turned[:, count:] = theirs_ref[:, lanes].T
            low = pl.ds(pl.multiple_of(spots_ref[1, part], 16), rows)
            left[part * rows : (part + 1) * rows] = turned[low]

    total[...] = mat(left[:, :count], grad_ref[...], NN) + mat(left[:, count:], other_ref[...], NN)
    for part, out in enumerate(outs):
        first = part * rows
        if out.shape[0] == half:
            first = pl.multiple_of(first + spots_ref[2, 0] * half, 8)
        out[...] = total[pl.ds(first, out.shape[0]), :].astype(out.dtype)


def grad_parts(mine, theirs, grad, other, chips):
    (count, columns), features = grad.shape, mine.shape[1]
    rows = 2 * features // lax.axis_size("fsdp")
    reach = (rows + 128 - gcd(rows, 128) + 127) // 128 * 128
    starts = jnp.stack([jnp.asarray(chip, jnp.int32) * rows for chip in chips])
    windows = jnp.minimum(starts // 128, (features - reach) // 128)
    core = jnp.broadcast_to(lax.axis_index("fsdp") % 2, starts.shape)
    spots = jnp.stack([windows, starts - windows * 128, core.astype(jnp.int32)])
    tile, number = 1152 if columns > 2304 else 384, len(chips)
    if columns % tile:
        tile = 256
    tall = pl.BlockSpec((count, features), lambda i: (0, 0), pipeline_mode=pl.Buffered(1))
    wide = pl.BlockSpec((count, tile), lambda i: (0, i))
    kept = [rows // 2] + [rows] * (number - 2) + [rows // 2]
    kinds = [jnp.bfloat16] + [jnp.float32] * (number - 1)
    return pl.pallas_call(
        parts_kernel,
        out_shape=[jax.ShapeDtypeStruct((k, columns), kind) for k, kind in zip(kept, kinds)],
        grid=(columns // tile,),
        in_specs=[pl.BlockSpec(memory_space=pltpu.SMEM), tall, tall, wide, wide],
        out_specs=[pl.BlockSpec((k, tile), lambda i: (0, i)) for k in kept],
        scratch_shapes=[
            pltpu.VMEM((reach, 2 * count), jnp.bfloat16),
            pltpu.VMEM((number * rows, 2 * count), jnp.bfloat16),
            pltpu.VMEM((number * rows, tile), jnp.float32),
        ],
        compiler_params=pltpu.CompilerParams(vmem_limit_bytes=48 << 20),
        cost_estimate=pl.CostEstimate(
            flops=4 * number * rows * count * columns,
            transcendentals=0,
            bytes_accessed=4 * count * (columns + features) + 4 * (number - 1) * rows * columns,
        ),
    )(spots, mine, theirs, grad, other)


def core_hop(block):
    chips = lax.axis_size("fsdp") // 2
    route = ring_route(chips)
    pairs = []
    for spot, chip in enumerate(route):
        for core, way in ((0, 1), (1, -1)):
            pairs.append((2 * chip + core, 2 * route[(spot + way) % chips] + core))
    return lax.ppermute(block, "fsdp", pairs)


def bins_sum(part):
    across = yield bins_peer, part
    return part.astype(jnp.float32) + across.astype(jnp.float32)


def grad_chain(pairs, theirs):
    heights = [left.shape[1] // lax.axis_size("fsdp") for left, _ in pairs]
    if any(rows % 8 for rows in heights):
        return [full_grad(left, right) for left, right in pairs]
    core = lax.axis_index("fsdp") % 2
    way = 1 - 2 * core
    far = lax.axis_size("fsdp") // 4
    others = yield each([core_swap] * len(pairs)), [right for _, right in pairs]
    steps = list(range(far, 0, -1))
    chips = [chip_at(far)] + [chip_at(way * apart) for apart in steps[1:]] + [chip_at(0)]
    parts = [
        grad_parts(left, peer, right, other, chips)
        for (left, right), peer, other in zip(pairs, theirs, others)
    ]

    def joined(blocks):
        return blocks[0] if len(blocks) == 1 else jnp.concatenate(blocks)

    def split(block, times):
        out, top = [], 0
        for rows in heights:
            out.append(block[top : top + times * rows])
            top += times * rows
        return out

    arrived = yield core_hop, joined([part[0] for part in parts])
    for number in range(1, far):
        if number == 1:
            spread = []
            for half in split(arrived, 1):
                spread += [jnp.where(core == 0, half, 0), jnp.where(core == 0, 0, half)]
            arrived = jnp.concatenate(spread)
        sums = [part[number] + block for part, block in zip(parts, split(arrived, 2))]
        arrived = yield core_hop, joined([block.astype(jnp.bfloat16) for block in sums])
    kept = [lax.dynamic_slice_in_dim(block, core * rows, rows) for block, rows in zip(split(arrived, 2), heights)]
    sent = [lax.dynamic_slice_in_dim(block, (1 - core) * rows, rows) for block, rows in zip(split(arrived, 2), heights)]
    back = yield core_swap, joined(sent)
    rounded = [
        lax.reduce_precision(part[far] + mine + more, 8, 7)
        for part, mine, more in zip(parts, kept, split(back, 1))
    ]
    across = yield bins_peer, joined([block.astype(jnp.bfloat16) for block in rounded])
    return [block + more.astype(jnp.float32) for block, more in zip(rounded, split(across, 1))]


class Chain:
    def __init__(self, steps):
        self.steps, self.flight, self.result = steps, (), None
        self.take(None)
        self.launch()

    def take(self, arrived):
        try:
            self.send, self.block = self.steps.send(arrived)
        except StopIteration as stop:
            self.send, self.block, self.result = None, None, stop.value

    def launch(self):
        self.flight = None if self.send is None else self.send(self.block)

    def push(self):
        if self.flight is not None:
            self.take(self.flight)
            self.launch()

    def finish(self):
        while self.flight is not None:
            self.push()
        return self.result


def arrive(values, *chains):
    chains = [chain for chain in chains if chain.flight is not None]
    if not chains:
        return values
    values, flights = lax.optimization_barrier((values, [chain.flight for chain in chains]))
    for chain, flight in zip(chains, flights):
        chain.take(flight)
    return values


def depart(values, *chains):
    ready = [(chain.block, chain.result) for chain in chains]
    values, ready = lax.optimization_barrier((values, ready))
    for chain, (chain.block, chain.result) in zip(chains, ready):
        chain.launch()
    return values


def beats(values, *chains):
    chains = [chain for chain in chains if chain.flight is not None]
    return depart(arrive(values, *chains), *chains) if chains else values


def full_grad(left, right):
    return both_groups(ring_sum(chip_grad(left, right)))


def modulate(values, shift, scale):
    center = values - jnp.mean(values, axis=-1, keepdims=True)
    spread = jnp.mean(center * center, axis=-1, keepdims=True)
    return center * lax.rsqrt(spread + 1e-06) * (1.0 + scale) + shift


def cosine_sum(target_f, predicted):
    dots = jnp.sum(predicted * target_f, axis=-1)
    first = lax.rsqrt(jnp.sum(predicted * predicted, axis=-1) + 1e-06)
    second = lax.rsqrt(jnp.sum(target_f * target_f, axis=-1) + 1e-06)
    return jnp.sum(dots * first * second)


def product(left, right):
    return jnp.dot(left, right, preferred_element_type=jnp.float32)


def input_grad(grad, weight):
    return jnp.einsum("ne,de->nd", grad, weight, preferred_element_type=jnp.float32)


def shards(
    tokens,
    condition,
    segments,
    cotangent,
    target,
    w_ada,
    w_qkv,
    w_out,
    w_fc1,
    w_fc2,
    w_proj1,
    w_proj2,
    w_proj3,
):
    count = tokens.shape[0]
    width = tokens.shape[1]
    head_size = width // HEADS
    factor = head_size ** (-0.5)
    tokens_f = tokens.astype(jnp.float32)
    target_f = target.astype(jnp.float32)
    silu_cond, silu_back = jax.vjp(jax.nn.silu, condition)
    cond_low = silu_cond.astype(jnp.bfloat16)
    mod_cols = product(cond_low, w_ada)
    first_set = Chain(whole([w_qkv, w_out], width))
    mod_chain = Chain(doubled(mod_cols.reshape(-1)))
    for _ in range(2):
        first_set.push()
        mod_chain.push()
    w_fc1, w_fc2, w_proj3 = beats((w_fc1, w_fc2, w_proj3), first_set)
    second_set = Chain(whole([w_fc1, w_fc2], width))
    head_third = lax.all_gather(w_proj3, "fsdp", axis=0, tiled=True)
    modulation = mod_chain.finish().reshape(6, width)
    full_qkv, full_out = first_set.finish()
    full_qkv, full_out = beats((full_qkv, full_out), second_set)
    h_one, norm_one_back = jax.vjp(modulate, tokens_f, modulation[0], modulation[1])
    in_one = h_one.astype(jnp.bfloat16)
    qkv_low = product(in_one, full_qkv).astype(jnp.bfloat16)
    peer_low = swapped(qkv_low[:, width:], "fsdp", 0)
    qkv_low, peer_low, w_proj1, w_proj2 = beats(
        (qkv_low, peer_low, w_proj1, w_proj2), second_set
    )
    third_set = Chain(whole([w_proj1, w_proj2], w_proj1.shape[1] // 2))
    place = lax.axis_index("fsdp")
    own_ids = lax.dynamic_slice_in_dim(segments, place * count, count)
    long = (own_ids[:1] == own_ids[count - 1 :]).astype(jnp.int32)
    attended, exact, _, logs = attend(long, qkv_low, peer_low, factor)
    attended, exact, logs = beats((attended, exact, logs), second_set)
    attended, exact, logs = beats((attended, exact, logs), third_set)
    branch_one = product(attended, full_out)
    resid_one = tokens_f + modulation[2] * branch_one
    resid_one = beats(resid_one, second_set)
    resid_one = beats(resid_one, third_set)
    full_fc1, full_fc2 = second_set.finish()
    full_fc1, full_fc2 = beats((full_fc1, full_fc2), third_set)
    h_two, norm_two_back = jax.vjp(modulate, resid_one, modulation[3], modulation[4])
    in_two = h_two.astype(jnp.bfloat16)
    hidden_pre = product(in_two, full_fc1)
    hidden_act, gelu_back = jax.vjp(partial(jax.nn.gelu, approximate=True), hidden_pre)
    hidden_low = hidden_act.astype(jnp.bfloat16)
    hidden_low = beats(hidden_low, third_set)
    branch_two = product(hidden_low, full_fc2)
    result = resid_one + modulation[5] * branch_two
    result_low = result.astype(jnp.bfloat16)
    head_first, head_second = third_set.finish()
    first_act, first_back = jax.vjp(jax.nn.silu, product(result_low, head_first))
    first_low = first_act.astype(jnp.bfloat16)
    second_act, second_back = jax.vjp(jax.nn.silu, product(first_low, head_second))
    second_low = second_act.astype(jnp.bfloat16)
    predicted = product(second_low, head_third)
    cos_total, cos_back = jax.vjp(partial(cosine_sum, target_f), predicted)
    in_one_peer, in_two_peer, attended_peer, hidden_peer = (
        swapped(block, "fsdp", 0) for block in (in_one, in_two, attended, hidden_low)
    )
    (grad_pred,) = cos_back(jnp.float32(-1.0))
    grad_pred_low = grad_pred.astype(jnp.bfloat16)
    total_third = low_grad(second_low, grad_pred_low)
    grad_pred_low, total_third = lax.optimization_barrier((grad_pred_low, total_third))
    part_third = scattered(total_third)
    (grad_second_pre,) = second_back(input_grad(grad_pred_low, head_third))
    grad_second_low = grad_second_pre.astype(jnp.bfloat16)
    total_second = low_grad(first_low, grad_second_low)
    grad_second_low, total_second = lax.optimization_barrier((grad_second_low, total_second))
    part_second = scattered(total_second)
    (grad_first_pre,) = first_back(input_grad(grad_second_low, head_second))
    grad_first_low = grad_first_pre.astype(jnp.bfloat16)
    d_result = cotangent.astype(jnp.float32) + input_grad(grad_first_low, head_first)
    total_first = low_grad(result_low, grad_first_low)
    d_result, total_first = lax.optimization_barrier((d_result, total_first))
    part_first = scattered(total_first)
    grad_gate_two = jnp.sum(d_result * branch_two, axis=0)
    d_branch_two = (d_result * modulation[5]).astype(jnp.bfloat16)
    chain_fc2 = Chain(grad_chain([(hidden_low, d_branch_two)], [hidden_peer]))
    (d_pre,) = gelu_back(input_grad(d_branch_two, full_fc2))
    d_pre_low = d_pre.astype(jnp.bfloat16)
    d_pre_low = beats(d_pre_low, chain_fc2)
    d_pre_low, part_third = lax.optimization_barrier((d_pre_low, part_third))
    chain_third = Chain(bins_sum(part_third))
    chain_fc1 = Chain(grad_chain([(in_two, d_pre_low)], [in_two_peer]))
    d_in_two = input_grad(d_pre_low, full_fc1)
    d_in_two = beats(d_in_two, chain_fc2)
    d_resid_part, grad_shift_two, grad_scale_two = norm_two_back(d_in_two)
    d_resid = d_result + d_resid_part
    grad_gate_one = jnp.sum(d_resid * branch_one, axis=0)
    d_branch_one = (d_resid * modulation[2]).astype(jnp.bfloat16)
    chain_out = Chain(grad_chain([(attended, d_branch_one)], [attended_peer]))
    d_branch_one = beats(d_branch_one, chain_fc1)
    d_attended = input_grad(d_branch_one, full_out).astype(jnp.bfloat16)
    d_attended = beats(d_attended, chain_out)
    d_attended = beats(d_attended, chain_fc2, chain_third)
    busy = [chain for chain in (chain_fc2, chain_fc1) if chain.flight is not None]
    d_queries, d_keys, d_values, d_peer = arrive(
        attend_back(long, qkv_low, peer_low, d_attended, exact, logs, factor), *busy
    )
    from_peer = swapped(d_peer, "fsdp", 0)
    d_queries = depart(d_queries, *busy)
    d_qkv = jnp.concatenate(
        [
            d_queries,
            (d_keys + from_peer[:, :width]).astype(jnp.bfloat16),
            (d_values + from_peer[:, width:]).astype(jnp.bfloat16),
        ],
        axis=1,
    )
    chain_qkv = Chain(grad_chain([(in_one, d_qkv)], [in_one_peer]))
    d_in_one = input_grad(d_qkv, full_qkv)
    d_in_one = beats(d_in_one, chain_qkv)
    d_in_one, part_second = lax.optimization_barrier((d_in_one, part_second))
    chain_second = Chain(bins_sum(part_second))
    d_tok_part, grad_shift_one, grad_scale_one = norm_one_back(d_in_one)
    d_modulation = jnp.stack(
        [
            grad_shift_one,
            grad_scale_one,
            grad_gate_one,
            grad_shift_two,
            grad_scale_two,
            grad_gate_two,
        ]
    ).reshape(6 * width)
    grad_tokens = d_resid + d_tok_part
    chain_mod = Chain(column_sums(d_modulation, w_ada))
    rounds = (
        (chain_fc2, chain_fc1, chain_out, chain_mod),
        (chain_qkv, chain_fc2, chain_mod, chain_second),
        (chain_fc1, chain_out, chain_mod),
        (chain_qkv, chain_mod),
        (chain_fc1, chain_out, chain_fc2, chain_mod),
        (chain_qkv, chain_fc1, chain_out, chain_mod),
    )
    for number, chains in enumerate(rounds):
        grad_tokens = beats(grad_tokens, *chains)
        if number == 2:
            grad_tokens, part_first = lax.optimization_barrier((grad_tokens, part_first))
            chain_first = Chain(bins_sum(part_first))
    grad_tokens = beats(grad_tokens, chain_qkv, chain_first, chain_mod)
    grad_tokens = beats(grad_tokens, chain_qkv, chain_fc1, chain_out, chain_mod)
    grad_first, grad_second, grad_third = (
        chain.finish() for chain in (chain_first, chain_second, chain_third)
    )
    mod_grad_cols, other_cols, cond_total = chain_mod.finish()
    (grad_qkv,), (grad_fc1,), (grad_out,), (grad_fc2,) = (
        chain.finish() for chain in (chain_qkv, chain_fc1, chain_out, chain_fc2)
    )
    (grad_condition,) = silu_back(cond_total)
    group = lax.axis_index("bins")
    cond_low_f = cond_low.astype(jnp.float32)
    other_cond = bins_peer(cond_low_f)
    first_cond = jnp.where(group == 0, cond_low_f, other_cond)
    last_cond = jnp.where(group == 0, other_cond, cond_low_f)
    first_cols = jnp.where(group == 0, mod_grad_cols, other_cols)
    last_cols = jnp.where(group == 0, other_cols, mod_grad_cols)
    grad_ada = first_cond.T * first_cols + last_cond.T * last_cols
    return (
        result_low,
        grad_tokens,
        grad_condition,
        grad_ada,
        grad_qkv,
        grad_out,
        grad_fc1,
        grad_fc2,
        grad_first,
        grad_second,
        grad_third,
    )


def solution(mesh):
    placed = (
        P(("bins", "fsdp"), None),
        P("bins", None),
        P("bins"),
        P(("bins", "fsdp"), None),
        P(("bins", "fsdp"), None),
        P(None, "fsdp"),
        P("fsdp", None),
        P("fsdp", None),
        P("fsdp", None),
        P("fsdp", None),
        P("fsdp", None),
        P("fsdp", None),
        P("fsdp", None),
    )
    return jax.shard_map(
        shards,
        mesh=mesh,
        in_specs=placed,
        out_specs=(
            P(("bins", "fsdp"), None),
            P(("bins", "fsdp"), None),
            P("bins", None),
            P(None, "fsdp"),
            P("fsdp", None),
            P("fsdp", None),
            P("fsdp", None),
            P("fsdp", None),
            P("fsdp", None),
            P("fsdp", None),
            P("fsdp", None),
        ),
        check_vma=False,
    )
```
